128 devices in a mesh: tok: 8 (over z, core), head: 16 (over y, x).
Axes of the slice: x: 4, y: 4, z: 4, core: 2. Of those that a mesh axis runs over, the one named last changes fastest.
Arguments:
- stream: bfloat16 [2048, 7168], P('tok'), may hold values from -400 to 400
- row_tree_nodes: int32 [2048], replicated, may hold values from 0 to 2047, as said below
- input_norm_gain: bfloat16 [7168], replicated, may hold values from 0.099609375 to 1.8984375
- query_key_value_weight: bfloat16 [7168, 3, 7168], P('head', None, 'tok'), may hold values from -0.141736677 to 0.141736677
- adapter_down_weight: bfloat16 [7168, 128], replicated, may hold values from -0.0625 to 0.0625
- adapter_up_weight: bfloat16 [128, 3, 7168], P('head', None, 'tok'), may hold values from -0.23925781 to 0.23925781
- key_value_cache: bfloat16 [2, 32, 2048, 7168], P(None, 'head', None, 'tok'), may hold values from -104 to 104
- cache_length: int32 [32], P('head'), may hold values from 256 to 2048, as said below
- parents: int32 [32, 64], P('head'), may hold values from 0 to 62, as said below
- accepted: int32 [32, 8], P('head'), may hold values from 0 to 63, as said below
- output_weight: bfloat16 [7168, 3584], P('tok', 'head'), may hold values from -0.375 to 0.375
Outputs:
- attended: bfloat16 [2048, 3584], P('tok', 'head')
- accepted_kv: bfloat16 [2, 32, 8, 7168], P(None, 'head', None, 'tok')
The draws below stay inside these ranges and needn't reach their ends.
Inputs may be any that keep to these rules, and one draw needn't show every extreme that they name: row_tree_nodes is a permutation of the 2048 node numbers; every aligned block of 128 rows holds exactly 4 nodes of every request. `cache_length`: at least one request's cache holds exactly 2048 positions. parents[r, 0] = 0 marks the root; parents[r, n] < n for n > 0. `accepted`: each row lists 8 nodes of its request's tree, each the parent of the next.
All inputs are finite; a program needn't handle non-finite values.
Results may differ from the reference program's by a relative error of at most 0.014.
Values may be sent and summed in bfloat16 or wider, within the bound.
A program may use at most 192 MiB of HBM per device.

```python
import math
import jax
import jax.numpy as jnp
from jax import lax

D = 3584
HEAD_COUNT = 32
HEAD_SIZE = 224
ADAPTER_RANK = 128
NODES = 64
DEPTH = 8
REQ_DEV = 2
CACHE = 2048
INPUT_WIDTH = 7168
REQ = 32
TOKENS = 2048


def draw_stream(key, part):
    base_key, row_key, column_key = jax.random.split(key, 3)
    row_scale = jnp.exp(jax.random.uniform(row_key, (TOKENS, 1), jnp.float32, 0.0, math.log(10.0)))
    column_scale = jnp.exp(jax.random.uniform(column_key, (1, INPUT_WIDTH), jnp.float32, 0.0, math.log(10.0)))
    core = jnp.clip(jax.random.normal(base_key, (TOKENS, INPUT_WIDTH), jnp.float32), -4.0, 4.0)
    return (core * row_scale * column_scale).astype(jnp.bfloat16)


def draw_row_tree_nodes(key, part):
    owners = REQ // REQ_DEV
    share_count = NODES // owners
    order_key, shuffle_key = jax.random.split(key)
    orders = jax.vmap(lambda one_key: jax.random.permutation(one_key, NODES))(jax.random.split(order_key, REQ))
    node_ids = orders.astype(jnp.int32) + (jnp.arange(REQ, dtype=jnp.int32) * NODES)[:, None]
    grouped = node_ids.reshape(REQ, owners, share_count).transpose(1, 0, 2).reshape(owners, REQ * share_count)
    shuffles = jax.vmap(lambda one_key: jax.random.permutation(one_key, REQ * share_count))(jax.random.split(shuffle_key, owners))
    return jnp.take_along_axis(grouped, shuffles.astype(jnp.int32), axis=1).reshape(TOKENS).astype(jnp.int32)


def draw_query_key_value_weight(key, part):
    slot_scale = jnp.array([1.0, 3.0, 1.0], jnp.float32)[None, :, None] * INPUT_WIDTH ** (-0.5)
    base = jnp.clip(jax.random.normal(key, (INPUT_WIDTH, 3, HEAD_COUNT * HEAD_SIZE), jnp.float32), -4.0, 4.0)
    return (base * slot_scale).astype(jnp.bfloat16)


def draw_key_value_cache(key, part):
    key_key, value_key = jax.random.split(key, 2)
    target_shape = (REQ, CACHE, HEAD_COUNT * HEAD_SIZE)
    keys_part = jnp.clip(jax.random.normal(key_key, target_shape, jnp.float32), -4.0, 4.0)
    values_part = jnp.clip(jax.random.normal(value_key, target_shape, jnp.float32), -4.0, 4.0)
    return jnp.stack([keys_part, values_part]).astype(jnp.bfloat16)


def draw_cache_length(key, part):
    length_key, full_key = jax.random.split(key)
    lengths = jax.random.randint(length_key, (REQ,), CACHE // 8, CACHE + 1)
    full_slot = jax.random.randint(full_key, (), 0, REQ)
    return jnp.where(jnp.arange(REQ) == full_slot, CACHE, lengths).astype(jnp.int32)


def tree_walk(key):
    tree_key = jax.random.fold_in(key, 11)
    back_key, leaf_key = jax.random.split(tree_key)
    steps_back = jax.random.randint(back_key, (REQ, NODES), 0, 4)
    positions = jnp.arange(NODES, dtype=jnp.int32)[None, :]
    parent_table = jnp.maximum(positions - 1 - steps_back, 0).astype(jnp.int32)
    leaves = jax.random.randint(leaf_key, (REQ,), NODES - 4, NODES).astype(jnp.int32)
    path_nodes = [leaves]
    for depth_step in range(DEPTH - 1):
        path_nodes.append(jnp.take_along_axis(parent_table, path_nodes[-1][:, None], axis=1)[:, 0])
    accepted_path = jnp.stack(path_nodes[::-1], axis=1).astype(jnp.int32)
    return (parent_table, accepted_path)


def draw_parents(key, part):
    return tree_walk(key)[0]


def draw_accepted(key, part):
    return tree_walk(key)[1]


def block_scale(stream_key, shape, cuts, smallest, high):
    level = 1.0
    for axis_at, parts in cuts:
        steps = jax.random.uniform(jax.random.fold_in(jax.random.fold_in(stream_key, 6), axis_at), (parts,), jnp.float32, smallest / len(cuts), high / len(cuts))
        level = level * jnp.repeat(jnp.exp(steps), shape[axis_at] // parts).reshape((-1,) + (1,) * (len(shape) - 1 - axis_at))
    return level


def bell_draw(own_key, shape, width, most, cuts=(), kind=jnp.bfloat16):
    result = jax.random.normal(own_key, shape, jnp.float32) * width
    if len(cuts) > 0:
        result = block_scale(own_key, shape, cuts, -0.22, 0.18) * result
    return jnp.clip(result, min=-most, max=most).astype(kind)


def setup_inputs(seed: int = 0) -> dict:
    key_list = jax.random.split(jax.random.key(seed), 12)
    return {
        "stream": draw_stream(jax.random.fold_in(key_list[11], 71), 0),
        "row_tree_nodes": draw_row_tree_nodes(jax.random.fold_in(key_list[11], 71), 0),
        "input_norm_gain": jnp.clip(1.0 + 0.18 * jax.random.normal(key_list[2], (INPUT_WIDTH,), jnp.float32), 0.099609375, 1.8984375).astype(jnp.bfloat16),
        "query_key_value_weight": draw_query_key_value_weight(jax.random.fold_in(key_list[11], 71), 0),
        "adapter_down_weight": bell_draw(key_list[4], (INPUT_WIDTH, ADAPTER_RANK), INPUT_WIDTH ** -0.5, 0.0625),
        "adapter_up_weight": bell_draw(key_list[5], (ADAPTER_RANK, 3, HEAD_COUNT * HEAD_SIZE), 0.04, 0.23925781, ((0, 16), (2, 8))),
        "key_value_cache": draw_key_value_cache(jax.random.fold_in(key_list[11], 71), 0),
        "cache_length": draw_cache_length(jax.random.fold_in(key_list[11], 71), 0),
        "parents": draw_parents(jax.random.fold_in(key_list[11], 71), 0),
        "accepted": draw_accepted(jax.random.fold_in(key_list[11], 71), 0),
        "output_weight": bell_draw(key_list[10], (HEAD_COUNT * HEAD_SIZE, D), HEAD_SIZE ** -0.5, 0.375, ((0, 8), (1, 16))),
    }


def ancestors_of(parents):
    parent_links = jax.nn.one_hot(parents, NODES, dtype=jnp.float32)
    identity_matrix = jnp.eye(NODES, dtype=jnp.float32)
    ancestry = jnp.minimum(identity_matrix[None] + parent_links, 1.0)
    for squaring in range(NODES.bit_length()):
        ancestry = jnp.minimum(jnp.einsum('rnm,rmk->rnk', ancestry, ancestry, precision=lax.Precision.HIGHEST), 1.0)
    return ancestry

def attend_one(request_item):
    queries, tree_key_rows, tree_value_rows, keys_cache, values_cache, length, ancestry = request_item
    attention_score_scale = HEAD_SIZE ** (-0.5)
    query_full_rows = queries.astype(jnp.float32)
    cache_scores = jnp.einsum('nhd,chd->hnc', query_full_rows, keys_cache.astype(jnp.float32)) * attention_score_scale
    live_mask = jnp.arange(CACHE) < length
    cache_scores = jnp.where(live_mask[None, None, :], cache_scores, -jnp.inf)
    tree_score_matrix = jnp.einsum('teo,ueo->etu', query_full_rows, tree_key_rows.astype(jnp.float32)) * attention_score_scale
    tree_score_matrix = jnp.where(ancestry[None] > 0.5, tree_score_matrix, -jnp.inf)
    largest = jnp.maximum(lax.optimization_barrier(jnp.max(cache_scores, axis=-1, keepdims=True)), lax.optimization_barrier(jnp.max(tree_score_matrix, axis=-1, keepdims=True)))
    cache_exp = jnp.exp(cache_scores - largest)
    tree_exp = jnp.exp(tree_score_matrix - largest)
    totals = lax.optimization_barrier(jnp.sum(cache_exp, axis=-1, keepdims=True)) + lax.optimization_barrier(jnp.sum(tree_exp, axis=-1, keepdims=True))
    cache_weights = (cache_exp / totals).astype(jnp.bfloat16)
    tree_weight_matrix = (tree_exp / totals).astype(jnp.bfloat16)
    final_output = jnp.einsum('hnc,chd->nhd', cache_weights.astype(jnp.float32), values_cache.astype(jnp.float32))
    final_output = final_output + jnp.einsum('ilf,fiz->liz', tree_weight_matrix.astype(jnp.float32), tree_value_rows.astype(jnp.float32))
    return final_output.astype(jnp.bfloat16)

def reference(stream, row_tree_nodes, input_norm_gain, query_key_value_weight, adapter_down_weight, adapter_up_weight, key_value_cache, cache_length, parents, accepted, output_weight):
    complete_width = HEAD_COUNT * HEAD_SIZE
    wide_rows = stream.astype(jnp.float32)
    inverse_rms = lax.rsqrt(lax.optimization_barrier(jnp.mean(wide_rows * wide_rows, axis=1, keepdims=True)) + 1e-05)
    normalized_input = (wide_rows * inverse_rms * input_norm_gain.astype(jnp.float32)).astype(jnp.bfloat16)
    reduced_rank_rows = jnp.dot(normalized_input, adapter_down_weight, preferred_element_type=jnp.float32).astype(jnp.bfloat16)
    query_key_value_sum = jnp.dot(normalized_input, query_key_value_weight.reshape(INPUT_WIDTH, 3 * complete_width), preferred_element_type=jnp.float32)
    query_key_value_sum = query_key_value_sum + jnp.dot(reduced_rank_rows, adapter_up_weight.reshape(ADAPTER_RANK, 3 * complete_width), preferred_element_type=jnp.float32)
    qkv = query_key_value_sum.astype(jnp.bfloat16)
    node_to_row = jnp.argsort(row_tree_nodes)
    node_qkv = qkv[node_to_row].reshape(REQ, NODES, 3, HEAD_COUNT, HEAD_SIZE)
    ancestry = ancestors_of(parents)
    keys_cache = key_value_cache[0].reshape(REQ, CACHE, HEAD_COUNT, HEAD_SIZE)
    values_cache = key_value_cache[1].reshape(REQ, CACHE, HEAD_COUNT, HEAD_SIZE)
    attention = lax.map(attend_one, (node_qkv[:, :, 0], node_qkv[:, :, 1], node_qkv[:, :, 2], keys_cache, values_cache, cache_length, ancestry))
    head_rows = attention.reshape(TOKENS, complete_width)[row_tree_nodes]
    attended = jnp.dot(head_rows, output_weight, preferred_element_type=jnp.float32).astype(jnp.bfloat16)
    node_table = node_qkv.reshape(REQ, NODES, 3, complete_width)
    chosen = jnp.take_along_axis(node_table, accepted[:, :, None, None], axis=1)
    accepted_kv = jnp.stack([chosen[:, :, 1], chosen[:, :, 2]])
    return (attended, accepted_kv)
```

```python
import functools

import jax
import jax.numpy as jnp
from jax import lax
from jax.experimental import pallas as pl
from jax.experimental.pallas import tpu as pltpu
from jax.sharding import PartitionSpec as P

MESH = pl.DeviceIdType.MESH
F32 = jnp.float32
BF16 = jnp.bfloat16

WIDTH = 7168
COLS = 896
HEAD = 224
LOCAL_HEADS = 4
RANK = 128
NODES = 64
ROWS = 256
KW = 512
UNITS = 12
LAG = 2
PIECE = 512
NEG = float("-inf")
NT = (((1,), (1,)), ((), ()))


def iota(shape, dim):
    return lax.broadcasted_iota(jnp.int32, shape, dim)


def mm(a, b):
    return jnp.dot(a, b, preferred_element_type=F32)


def column_of(row):
    n = row.shape[1]
    eye = iota((n, n), 0) == iota((n, n), 1)
    return jnp.sum(jnp.where(eye, jnp.broadcast_to(row, (n, n)), 0.0), axis=1, keepdims=True)


def row_of(col):
    n = col.shape[0]
    eye = iota((n, n), 0) == iota((n, n), 1)
    return jnp.sum(jnp.where(eye, jnp.broadcast_to(col, (n, n)), 0.0), axis=0, keepdims=True)


def one(mask):
    return jnp.where(mask, 1.0, 0.0).astype(BF16)


def kernel(
    stream_h, nodes, gain, wqkv_h, adown_h, aup, kv_h, clen, parents, accepted, wo_h,
    out_ref, akv_ref,
    stream_v, gain32, adown_v, low_acc, rstd_v, wbuf, kv_v, xbuf, wo_v, part,
    ra, rb, rc, rd, qkv, sort_p, node_q, node_qt, anc_v, qbd, acc_v, m_v, l_v, att, res,
    ld, x_s, x_r, w_s, w_r, rs_s, rs_r, aa_s, aa_r, g1_s, g1_r, g2_s, g2_r, g3_s, g3_r, g4_s, g4_r,
):
    t = lax.axis_index("tok")
    h = lax.axis_index("head")
    z, core = t // 2, t % 2
    y, x = h // 4, h % 4

    def hx(d):
        return y * 4 + (x + d + 4) % 4

    def hy(d):
        return ((y + d + 4) % 4) * 4 + x

    def tz(d, other=False):
        c = 1 - core if other else core
        return ((z + d + 4) % 4) * 2 + c

    xm, xp, x2 = (x + 3) % 4, (x + 1) % 4, (x + 2) % 4
    ym, yp, y2 = (y + 3) % 4, (y + 1) % 4, (y + 2) % 4

    def send(src, dst, ssem, rsem, axis, idx):
        pltpu.make_async_remote_copy(
            src_ref=src, dst_ref=dst, send_sem=ssem, recv_sem=rsem,
            device_id={axis: idx}, device_id_type=MESH,
        ).start()

    def wait(ref, sem):
        pltpu.make_async_copy(ref, ref, sem).wait()

    bar = pltpu.get_barrier_semaphore()
    for d in range(1, 8):
        pl.semaphore_signal(bar, inc=1, device_id={"tok": (t + d) % 8}, device_id_type=MESH)
    for idx in (hx(1), hx(-1), hy(1), hy(-1)):
        pl.semaphore_signal(bar, inc=1, device_id={"head": idx}, device_id_type=MESH)

    loads = []
    for r in range(4):
        c = pltpu.make_async_copy(
            stream_h.at[pl.ds(64 * r, 64)], stream_v.at[pl.ds(64 * r, 64)], ld.at[r]
        )
        c.start()
        loads.append(c)
    adown_c = pltpu.make_async_copy(adown_h, adown_v, ld.at[4])
    adown_c.start()
    odd = h % 2
    koff = pl.multiple_of(64 * odd, 64)
    foff = pl.multiple_of(448 * (1 - odd), 64)
    w_c = pltpu.make_async_copy(wqkv_h, wbuf.at[:, pl.ds(koff, 448), :], ld.at[5])
    w_c.start()
    wo_c = pltpu.make_async_copy(wo_h, wo_v.at[t], ld.at[6])
    wo_c.start()
    kv_c = pltpu.make_async_copy(kv_h, kv_v, ld.at[7])

    mine = nodes[pl.ds(2 * t, 2), :].astype(F32)
    key_row = jnp.concatenate([mine[0:1], mine[1:2]], axis=1)
    key_col = column_of(key_row)
    rank_row = jnp.sum(
        jnp.where(
            jnp.broadcast_to(key_col, (ROWS, ROWS)) < jnp.broadcast_to(key_row, (ROWS, ROWS)), 1.0, 0.0
        ),
        axis=0, keepdims=True,
    )
    sort_p[...] = one(iota((ROWS, ROWS), 0).astype(F32) == jnp.broadcast_to(rank_row, (ROWS, ROWS)))
    gain32[...] = gain[...].astype(F32)
    for p in range(3):
        up = aup[p].astype(F32)
        wbuf[p, pl.ds(foff, 64), :] = jnp.concatenate([up, jnp.zeros((56, COLS), F32)], axis=0).astype(BF16)

    for r in range(4):
        loads[r].wait()

        def sq(kk, acc, r=r):
            blk = stream_v[pl.ds(64 * r, 64), pl.ds(pl.multiple_of(1024 * kk, 1024), 1024)].astype(F32)
            blk = blk * blk
            for b in range(8):
                acc = acc + blk[:, 128 * b:128 * b + 128]
            return acc

        acc = lax.fori_loop(0, 7, sq, jnp.zeros((64, 128), F32))
        mean = jnp.sum(acc, axis=1, keepdims=True) * (1.0 / WIDTH)
        rstd_v[pl.ds(64 * r, 64), :] = jnp.broadcast_to(lax.rsqrt(mean + 1e-5), (64, 128))
    kv_c.start()
    adown_c.wait()
    low_acc[...] = jnp.zeros((ROWS, RANK), F32)

    def normed(block):
        xb = stream_v[:, pl.ds(pl.multiple_of(128 * block, 128), 128)].astype(F32)
        return (xb * rstd_v[...] * gain32[pl.ds(block, 1), :]).astype(BF16)

    def low_step(kk, carry):
        xn = jnp.concatenate([normed(8 * kk + b) for b in range(8)], axis=1)
        low_acc[...] += mm(xn, adown_v[pl.ds(pl.multiple_of(1024 * kk, 1024), 1024), :])
        return carry

    lax.fori_loop(0, 7, low_step, 0)
    first = (7 * h) // 2
    xw = jnp.concatenate([normed(first + b) for b in range(4)], axis=1)
    li = iota((RANK, KW), 1) - foff
    place = one((iota((RANK, KW), 0) - 8 * h == li) & (li >= 0) & (li < 8))
    low = mm(low_acc[...].astype(BF16), place).astype(BF16)
    lane = iota((ROWS, KW), 1) - foff
    xw = jnp.where((lane >= 0) & (lane < 64), low.astype(F32), xw.astype(F32)).astype(BF16)
    xbuf[t] = mm(sort_p[...], xw).astype(BF16)

    pl.semaphore_wait(bar, 11)

    def ag_own(buf, ss, rr):
        own = buf.at[t]
        send(own, own, ss.at[0], rr.at[1], "tok", tz(1))
        send(own, own, ss.at[1], rr.at[2], "tok", tz(-1))
        send(own, own, ss.at[2], rr.at[0], "tok", tz(0, True))

    def ag_near(buf, ss, rr, half):
        a, b = tz(-1), tz(1)
        wait(buf.at[a], rr.at[1])
        piece = buf.at[a, pl.ds(0, half)]
        send(piece, piece, ss.at[3], rr.at[3], "tok", tz(1))
        send(buf.at[a], buf.at[a], ss.at[4], rr.at[4], "tok", tz(0, True))
        wait(buf.at[b], rr.at[2])
        piece = buf.at[b, pl.ds(half, half)]
        send(piece, piece, ss.at[5], rr.at[3], "tok", tz(-1))
        send(buf.at[b], buf.at[b], ss.at[6], rr.at[5], "tok", tz(0, True))

    def ag_far(buf, ss, rr):
        c = tz(2)
        wait(buf.at[c], rr.at[3])
        send(buf.at[c], buf.at[c], ss.at[7], rr.at[6], "tok", tz(0, True))

    def ag_drain(buf, ss, half):
        for i in (0, 1, 2):
            wait(buf.at[t], ss.at[i])
        wait(buf.at[t, pl.ds(0, half)], ss.at[3])
        wait(buf.at[t], ss.at[4])
        wait(buf.at[t, pl.ds(0, half)], ss.at[5])
        wait(buf.at[t], ss.at[6])
        wait(buf.at[t], ss.at[7])

    ag_own(xbuf, x_s, x_r)
    w_c.wait()

    def chip_of(u):
        k = u % 4
        return (z + jnp.where(k == 0, 0, jnp.where(k == 1, 3, jnp.where(k == 2, 1, 2)))) % 4

    def add2(a, b):
        return a.astype(F32) + b.astype(F32)

    def s_matmul(u):
        p, zz = u // 4, chip_of(u)
        for e in range(2):
            prod = mm(xbuf[2 * zz + e], wbuf[p])
            part[u, e] = prod.astype(BF16).reshape(4, 4, 16, COLS)
        ss, rr = rs_s.at[0, u], rs_r.at[0, u]
        send(part.at[u, 0, pl.ds(0, 2), x2], ra.at[u, 0, 0], ss, rr, "head", hx(1))
        send(part.at[u, 0, pl.ds(2, 2), x2], ra.at[u, 0, 1], ss, rr, "head", hx(-1))
        send(part.at[u, 1, y2, pl.ds(0, 2)], ra.at[u, 1, 0], ss, rr, "head", hy(1))
        send(part.at[u, 1, y2, pl.ds(2, 2)], ra.at[u, 1, 1], ss, rr, "head", hy(-1))

    def s_b1(u):
        wait(ra.at[u], rs_r.at[0, u])
        ss, rr = rs_s.at[1, u], rs_r.at[1, u]
        part[u, 0, 0:2, xp] = add2(part[u, 0, 0:2, xp], ra[u, 0, 0]).astype(BF16)
        send(part.at[u, 0, :, xp], rb.at[u, 0, 0], ss, rr, "head", hx(1))
        part[u, 0, 2:4, xm] = add2(part[u, 0, 2:4, xm], ra[u, 0, 1]).astype(BF16)
        send(part.at[u, 0, :, xm], rb.at[u, 0, 1], ss, rr, "head", hx(-1))
        part[u, 1, yp, 0:2] = add2(part[u, 1, yp, 0:2], ra[u, 1, 0]).astype(BF16)
        send(part.at[u, 1, yp], rb.at[u, 1, 0], ss, rr, "head", hy(1))
        part[u, 1, ym, 2:4] = add2(part[u, 1, ym, 2:4], ra[u, 1, 1]).astype(BF16)
        send(part.at[u, 1, ym], rb.at[u, 1, 1], ss, rr, "head", hy(-1))

    def s_a2(u):
        wait(rb.at[u], rs_r.at[1, u])
        ss, rr = rs_s.at[2, u], rs_r.at[2, u]
        part[u, 0, :, x] = (add2(part[u, 0, :, x], rb[u, 0, 0]) + rb[u, 0, 1].astype(F32)).astype(BF16)
        part[u, 1, y] = (add2(part[u, 1, y], rb[u, 1, 0]) + rb[u, 1, 1].astype(F32)).astype(BF16)
        lo, hi = pl.ds(0, 512), pl.ds(512, 384)
        send(part.at[u, 0, y2, x, :, lo], rc.at[u, 0, :, lo], ss, rr, "head", hy(1))
        send(part.at[u, 0, y2, x, :, hi], rc.at[u, 0, :, hi], ss, rr, "head", hy(-1))
        send(part.at[u, 1, y, x2, :, lo], rc.at[u, 1, :, lo], ss, rr, "head", hx(1))
        send(part.at[u, 1, y, x2, :, hi], rc.at[u, 1, :, hi], ss, rr, "head", hx(-1))

    def s_b2(u):
        wait(rc.at[u], rs_r.at[2, u])
        ss, rr = rs_s.at[3, u], rs_r.at[3, u]
        part[u, 0, yp, x, :, 0:512] = add2(part[u, 0, yp, x, :, 0:512], rc[u, 0, :, 0:512]).astype(BF16)
        send(part.at[u, 0, yp, x], rd.at[u, 0, 0], ss, rr, "head", hy(1))
        part[u, 0, ym, x, :, 512:896] = add2(part[u, 0, ym, x, :, 512:896], rc[u, 0, :, 512:896]).astype(BF16)
        send(part.at[u, 0, ym, x], rd.at[u, 0, 1], ss, rr, "head", hy(-1))
        part[u, 1, y, xp, :, 0:512] = add2(part[u, 1, y, xp, :, 0:512], rc[u, 1, :, 0:512]).astype(BF16)
        send(part.at[u, 1, y, xp], rd.at[u, 1, 0], ss, rr, "head", hx(1))
        part[u, 1, y, xm, :, 512:896] = add2(part[u, 1, y, xm, :, 512:896], rc[u, 1, :, 512:896]).astype(BF16)
        send(part.at[u, 1, y, xm], rd.at[u, 1, 1], ss, rr, "head", hx(-1))

    def s_fin(u):
        wait(rd.at[u], rs_r.at[3, u])
        p, zz = u // 4, chip_of(u)
        for e in range(2):
            total = add2(part[u, e, y, x], rd[u, e, 0]) + rd[u, e, 1].astype(F32)
            qkv[p, 2 * zz + e] = total.astype(BF16)

    def prepare():
        node_col = iota((128, 128), 0).astype(F32) + (128 * h).astype(F32)
        acc = jnp.zeros((128, 128), F32)
        for b in range(16):
            line = jnp.broadcast_to(nodes[b:b + 1, :].astype(F32), (128, 128))
            acc = acc + jnp.where(line == node_col, float(b // 2), 0.0)
        tok_col = jnp.sum(acc, axis=1, keepdims=True)
        tok_row = row_of(tok_col)
        before = (jnp.broadcast_to(tok_col, (128, 128)) == jnp.broadcast_to(tok_row, (128, 128))) & (
            iota((128, 128), 1) < iota((128, 128), 0)
        )
        pos_col = 16.0 * tok_col + jnp.sum(jnp.where(before, 1.0, 0.0), axis=1, keepdims=True)
        pos_row = row_of(pos_col)
        node_qt[...] = one(iota((128, 128), 1).astype(F32) == jnp.broadcast_to(pos_col, (128, 128)))
        node_q[...] = one(iota((128, 128), 0).astype(F32) == jnp.broadcast_to(pos_row, (128, 128)))
        for r in range(2):
            par = column_of(parents[r:r + 1, :].astype(F32))
            i0, i1 = iota((NODES, NODES), 0), iota((NODES, NODES), 1)
            anc = one((i0 == i1) | (i1.astype(F32) == jnp.broadcast_to(par, (NODES, NODES))))
            for _ in range(6):
                anc = jnp.minimum(mm(anc, anc), 1.0).astype(BF16)
            anc_v[r] = anc.astype(F32)
        m_v[...] = jnp.full(m_v.shape, NEG, F32)
        l_v[...] = jnp.zeros(l_v.shape, F32)
        acc_v[...] = jnp.zeros(acc_v.shape, F32)

    def in_nodes(p):
        return mm(node_qt[...], qkv[p].reshape(128, COLS))

    def spread_queries():
        q = in_nodes(0)
        head_of = iota((NODES, COLS), 1) // HEAD
        for r in range(2):
            qr = q[NODES * r:NODES * r + NODES]
            for j in range(LOCAL_HEADS):
                qbd[r, NODES * j:NODES * j + NODES, :] = jnp.where(head_of == j, qr, 0.0).astype(BF16)

    scale = HEAD ** -0.5

    def soften(r, s, values):
        m_old = m_v[r]
        m_new = jnp.maximum(m_old, jnp.broadcast_to(jnp.max(s, axis=1, keepdims=True), m_old.shape))
        shrink = jnp.exp(m_old - m_new)
        e = jnp.exp(s - m_new[:, 0:1])
        m_v[r] = m_new
        l_v[r] = l_v[r] * shrink + jnp.broadcast_to(jnp.sum(e, axis=1, keepdims=True), m_old.shape)
        acc_v[r] = acc_v[r] * shrink[:, 0:1] + mm(e.astype(BF16), values)

    def cache_piece(i):
        r, c = i // 4, i % 4
        here = pl.ds(pl.multiple_of(PIECE * c, PIECE), PIECE)
        s = lax.dot_general(qbd[r], kv_v[0, r, here, :], NT, preferred_element_type=F32) * scale
        live = iota((256, PIECE), 1) + PIECE * c < clen[r]
        soften(r, jnp.where(live, s, NEG), kv_v[1, r, here, :])

    last = UNITS + 4 * LAG
    start_att = 4 + 4 * LAG

    def body(it, carry):
        @pl.when(it < UNITS)
        def _():
            @pl.when(it == 0)
            def _():
                wait(xbuf.at[tz(0, True)], x_r.at[0])

            @pl.when(it == 1)
            def _():
                ag_near(xbuf, x_s, x_r, ROWS // 2)
                wait(xbuf.at[tz(-1, True)], x_r.at[4])

            @pl.when(it == 2)
            def _():
                ag_far(xbuf, x_s, x_r)
                wait(xbuf.at[tz(1, True)], x_r.at[5])

            @pl.when(it == 3)
            def _():
                wait(xbuf.at[tz(2, True)], x_r.at[6])

            s_matmul(it)

        for lag, stage in ((LAG, s_b1), (2 * LAG, s_a2), (3 * LAG, s_b2), (4 * LAG, s_fin)):
            @pl.when((it >= lag) & (it < UNITS + lag))
            def _(lag=lag, stage=stage):
                stage(it - lag)

        @pl.when(it == 3)
        def _():
            wo_c.wait()
            ag_own(wo_v, w_s, w_r)

        @pl.when(it == 4)
        def _():
            prepare()

        @pl.when(it == 7)
        def _():
            ag_near(wo_v, w_s, w_r, HEAD // 2)

        @pl.when(it == 9)
        def _():
            ag_far(wo_v, w_s, w_r)

        @pl.when(it == start_att)
        def _():
            kv_c.wait()
            spread_queries()

        @pl.when((it >= start_att) & (it < start_att + 8))
        def _():
            cache_piece(it - start_att)

        return carry

    lax.fori_loop(0, last, body, 0)

    k_n, v_n = in_nodes(1).astype(BF16), in_nodes(2).astype(BF16)
    outs = []
    for r in range(2):
        rows = slice(NODES * r, NODES * r + NODES)
        s = lax.dot_general(qbd[r], k_n[rows], NT, preferred_element_type=F32) * scale
        keep = jnp.concatenate([anc_v[r]] * LOCAL_HEADS, axis=0) > 0.5
        soften(r, jnp.where(keep, s, NEG), v_n[rows])
        norm = acc_v[r] / l_v[r][:, 0:1]
        head_of = iota((NODES, COLS), 1) // HEAD
        o = jnp.zeros((NODES, COLS), F32)
        for j in range(LOCAL_HEADS):
            o = jnp.where(head_of == j, norm[NODES * j:NODES * j + NODES], o)
        outs.append(o.astype(BF16))
    att[...] = mm(node_q[...], jnp.concatenate(outs, axis=0)).astype(BF16).reshape(8, 16, COLS)

    for d in range(1, 8):
        to = (t + d) % 8
        send(att.at[to], res.at[t, h], aa_s.at[d - 1], aa_r.at[d - 1], "tok", to)
    res[t, h] = att[t]
    for r in range(2):
        col = column_of(accepted[r:r + 1, :].astype(F32)) + float(NODES * r)
        pick = one(iota((8, 128), 1).astype(F32) == jnp.broadcast_to(col, (8, 128)))
        akv_ref[0, r] = mm(pick, k_n).astype(BF16)
        akv_ref[1, r] = mm(pick, v_n).astype(BF16)
    for d in range(1, 8):
        wait(res.at[(t - d + 8) % 8, h], aa_r.at[d - 1])

    steps = (0, -1, 1, 2)

    def slot(hf, i, j):
        if hf == 0:
            return ((y + j + 4) % 4) * 4 + (x + i + 4) % 4
        return ((y + i + 4) % 4) * 4 + (x + j + 4) % 4

    def blk(hf, i, j, part_of=None):
        lo, n = (4 * hf, 4) if part_of is None else (4 * hf + 2 * part_of, 2)
        return res.at[pl.ds(lo, n), slot(hf, i, j)]

    def dev(hf, axis, d):
        return slot(hf, d, 0) if axis == 0 else slot(hf, 0, d)

    def first_sends(hf):
        for n, d in enumerate((1, -1)):
            send(blk(hf, 0, 0), blk(hf, 0, 0), g1_s.at[hf, n], g1_r.at[hf, n], "head", dev(hf, 0, d))

    def cross_sends(hf, n_i):
        i = steps[n_i]
        for n, d in enumerate((1, -1)):
            send(blk(hf, i, 0), blk(hf, i, 0), g3_s.at[hf, n_i, n], g3_r.at[hf, n_i, n], "head", dev(hf, 1, d))

    def cross_forward(hf, n_i):
        i = steps[n_i]
        for n, d in enumerate((1, -1)):
            wait(blk(hf, i, -d), g3_r.at[hf, n_i, n])
            send(blk(hf, i, -d, n), blk(hf, i, -d, n), g4_s.at[hf, n_i, n], g4_r.at[hf, n_i], "head", dev(hf, 1, d))

    for hf in range(2):
        first_sends(hf)
    for hf in range(2):
        cross_sends(hf, 0)
    for hf in range(2):
        for n, d in enumerate((1, -1)):
            wait(blk(hf, -d, 0), g1_r.at[hf, n])
            send(blk(hf, -d, 0, n), blk(hf, -d, 0, n), g2_s.at[hf, n], g2_r.at[hf], "head", dev(hf, 0, d))
            cross_sends(hf, 1 + n)
    for hf in range(2):
        cross_forward(hf, 0)
    for hf in range(2):
        wait(blk(hf, 2, 0), g2_r.at[hf])
        cross_sends(hf, 3)
    for n_i in (1, 2, 3):
        for hf in range(2):
            cross_forward(hf, n_i)

    ag_drain(xbuf, x_s, ROWS // 2)
    ag_drain(wo_v, w_s, HEAD // 2)
    for i, c in ((0, tz(0, True)), (4, tz(-1, True)), (5, tz(1, True)), (6, tz(2, True))):
        wait(wo_v.at[c], w_r.at[i])

    def drain(u, carry):
        for k, ref in enumerate((ra, rb, rc, rd)):
            wait(ref.at[u], rs_s.at[k, u])
        return carry

    lax.fori_loop(0, UNITS, drain, 0)
    for hf in range(2):
        for n_i in range(4):
            wait(blk(hf, steps[n_i], 2), g4_r.at[hf, n_i])

    total = jnp.zeros((HEAD, ROWS), F32)
    for s in range(8):
        total = total + lax.dot_general(
            wo_v[s], res[s].reshape(ROWS, COLS), NT, preferred_element_type=F32
        )
    out_ref[...] = mm(total.astype(BF16), sort_p[...]).astype(BF16)

    for d in range(1, 8):
        wait(att.at[0], aa_s.at[d - 1])
    for hf in range(2):
        for n in range(2):
            wait(blk(hf, 0, 0), g1_s.at[hf, n])
            wait(blk(hf, 0, 0, 0), g2_s.at[hf, n])
            for n_i in range(4):
                wait(blk(hf, 0, 0), g3_s.at[hf, n_i, n])
                wait(blk(hf, 0, 0, 0), g4_s.at[hf, n_i, n])


def on_device(stream, row_tree_nodes, gain, wqkv, adown, aup, kv, clen, parents, accepted, wo):
    vm = pl.BlockSpec(memory_space=pltpu.VMEM)
    hbm = pl.BlockSpec(memory_space=pl.ANY)
    sm = pl.BlockSpec(memory_space=pltpu.SMEM)
    dma = pltpu.SemaphoreType.DMA
    v = pltpu.VMEM
    out_t, akv = pl.pallas_call(
        kernel,
        out_shape=(
            jax.ShapeDtypeStruct((HEAD, ROWS), BF16),
            jax.ShapeDtypeStruct((2, 2, 8, COLS), BF16),
        ),
        in_specs=[hbm, vm, vm, hbm, hbm, vm, hbm, sm, vm, vm, hbm],
        out_specs=(vm, vm),
        scratch_shapes=[
            v((ROWS, WIDTH), BF16), v((56, 128), F32), v((WIDTH, RANK), BF16), v((ROWS, RANK), F32),
            v((ROWS, 128), F32), v((3, KW, COLS), BF16), v((2, 2, 2048, COLS), BF16), v((8, ROWS, KW), BF16),
            v((8, HEAD, COLS), BF16), v((UNITS, 2, 4, 4, 16, COLS), BF16),
            v((UNITS, 2, 2, 2, 16, COLS), BF16), v((UNITS, 2, 2, 4, 16, COLS), BF16),
            v((UNITS, 2, 16, COLS), BF16), v((UNITS, 2, 2, 16, COLS), BF16),
            v((3, 8, 16, COLS), BF16), v((ROWS, ROWS), BF16), v((128, 128), BF16), v((128, 128), BF16),
            v((2, NODES, NODES), F32), v((2, 256, COLS), BF16), v((2, 256, COLS), F32),
            v((2, 256, 128), F32), v((2, 256, 128), F32), v((8, 16, COLS), BF16), v((8, 16, 16, COLS), BF16),
            dma((8,)), dma((8,)), dma((7,)), dma((8,)), dma((7,)), dma((4, UNITS)), dma((4, UNITS)),
            dma((7,)), dma((7,)), dma((2, 2)), dma((2, 2)), dma((2, 2)), dma((2,)),
            dma((2, 4, 2)), dma((2, 4, 2)), dma((2, 4, 2)), dma((2, 4)),
        ],
        compiler_params=pltpu.CompilerParams(
            collective_id=0, has_side_effects=True, vmem_limit_bytes=67043328
        ),
        name="tree_verify",
    )(
        stream, row_tree_nodes.reshape(16, 128), gain.reshape(56, 128), jnp.transpose(wqkv, (1, 0, 2)),
        adown, jnp.transpose(aup, (1, 0, 2)), kv, clen, parents, accepted, jnp.transpose(wo),
    )
    return jnp.transpose(out_t), akv


def solution(mesh):
    placed = (
        P("tok", None), P(), P(), P("head", None, "tok"), P(), P("head", None, "tok"),
        P(None, "head", None, "tok"), P("head"), P("head", None), P("head", None), P("tok", "head"),
    )
    return jax.shard_map(
        on_device, mesh=mesh, in_specs=placed,
        out_specs=(P("tok", "head"), P(None, "head", None, "tok")), check_vma=False,
    )
```

```python
import functools

import jax
import jax.numpy as jnp
from jax import lax
from jax.experimental import pallas as pl
from jax.experimental.pallas import tpu as pltpu
from jax.sharding import PartitionSpec as P

MESH = pl.DeviceIdType.MESH
F32 = jnp.float32
BF16 = jnp.bfloat16

WIDTH = 7168
COLS = 896
HEAD = 224
LOCAL_HEADS = 4
RANK = 128
NODES = 64
ROWS = 256
KW = 512
UNITS = 12
LAG = 1
ASPLIT = 512
SENT = 464
PIECE = 512
NEG = float("-inf")
NT = (((1,), (1,)), ((), ()))


def iota(shape, dim):
    return lax.broadcasted_iota(jnp.int32, shape, dim)


def mm(a, b):
    return jnp.dot(a, b, preferred_element_type=F32)


def column_of(row):
    n = row.shape[1]
    eye = iota((n, n), 0) == iota((n, n), 1)
    return jnp.sum(jnp.where(eye, jnp.broadcast_to(row, (n, n)), 0.0), axis=1, keepdims=True)


def row_of(col):
    n = col.shape[0]
    eye = iota((n, n), 0) == iota((n, n), 1)
    return jnp.sum(jnp.where(eye, jnp.broadcast_to(col, (n, n)), 0.0), axis=0, keepdims=True)


def one(mask):
    return jnp.where(mask, 1.0, 0.0).astype(BF16)


def kernel(
    stream_h, nodes, gain, wqkv_h, adown_h, aup, kv_h, clen, parents, accepted, wo_h,
    out_ref, akv_ref,
    stream_v, gain32, adown_v, low_acc, rstd_v, wbuf, wa, wb, kv_v, xbuf, pack, wo_v, part,
    ra, rb, rc, rd, qkv, sort_p, node_q, node_qt, anc_v, qbd, acc_v, m_v, l_v, att, res,
    ld, x_s, x_r, w_s, w_r, p_s, p_r, rs_s, rs_r, aa_s, aa_r, g1_s, g1_r, g2_s, g2_r, g3_s, g3_r, g4_s, g4_r,
):
    t = lax.axis_index("tok")
    h = lax.axis_index("head")
    z, core = t // 2, t % 2
    y, x = h // 4, h % 4

    def hx(d):
        return y * 4 + (x + d + 4) % 4

    def hy(d):
        return ((y + d + 4) % 4) * 4 + x

    c1, c2 = jnp.where(core == 0, x, y), jnp.where(core == 0, y, x)
    par = c2 % 2

    def dev1(d):
        return jnp.where(core == 0, hx(d), hy(d))

    def dev2(d):
        return jnp.where(core == 0, hy(d), hx(d))

    dev_a = jnp.where(par == 0, dev2(1), dev2(-1))
    dev_b = jnp.where(par == 0, dev2(-1), dev2(1))

    def tz(d, other=False):
        c = 1 - core if other else core
        return ((z + d + 4) % 4) * 2 + c

    cm, cp, cf = (c1 + 3) % 4, (c1 + 1) % 4, (c1 + 2) % 4
    own_v = c2 // 2
    far_v = 1 - own_v

    def slot_of(tok):
        dz, same = (tok // 2 - z + 4) % 4, tok % 2 == core
        near = jnp.where(same, 2, 4) + jnp.where(dz == 1, 1, 0)
        far = jnp.where(same, 6, 7)
        return jnp.where(dz == 0, tok % 2, jnp.where(dz == 2, far, near))

    def send(src, dst, ssem, rsem, axis, idx):
        pltpu.make_async_remote_copy(
            src_ref=src, dst_ref=dst, send_sem=ssem, recv_sem=rsem,
            device_id={axis: idx}, device_id_type=MESH,
        ).start()

    def wait(ref, sem):
        pltpu.make_async_copy(ref, ref, sem).wait()

    loads = []
    for r in range(4):
        c = pltpu.make_async_copy(
            stream_h.at[pl.ds(64 * r, 64)], stream_v.at[pl.ds(64 * r, 64)], ld.at[r]
        )
        c.start()
        loads.append(c)
    adown_c = pltpu.make_async_copy(adown_h, adown_v, ld.at[4])
    adown_c.start()
    odd = h % 2
    koff = pl.multiple_of(64 * odd, 64)
    foff = pl.multiple_of(448 - 400 * odd, 16)
    sent = pl.ds(pl.multiple_of(48 * odd, 16), SENT)
    w_c = pltpu.make_async_copy(wqkv_h, wbuf.at[:, pl.ds(koff, 448), :], ld.at[5])
    w_c.start()
    wo_c = pltpu.make_async_copy(wo_h, wo_v.at[t], ld.at[6])
    wo_c.start()
    kv_c = pltpu.make_async_copy(kv_h, kv_v, ld.at[7])

    mine = nodes[pl.ds(2 * t, 2), :].astype(F32)
    key_row = jnp.concatenate([mine[0:1], mine[1:2]], axis=1)
    key_col = column_of(key_row)
    rank_row = jnp.sum(
        jnp.where(
            jnp.broadcast_to(key_col, (ROWS, ROWS)) < jnp.broadcast_to(key_row, (ROWS, ROWS)), 1.0, 0.0
        ),
        axis=0, keepdims=True,
    )
    sort_p[...] = one(iota((ROWS, ROWS), 0).astype(F32) == jnp.broadcast_to(rank_row, (ROWS, ROWS)))
    gain32[...] = gain[...].astype(F32)
    blank = jnp.zeros((48, COLS), BF16)
    for p in range(3):
        up = jnp.concatenate([aup[p].astype(F32), jnp.zeros((8, COLS), F32)], axis=0).astype(BF16)
        wbuf[p, pl.ds(pl.multiple_of(464 * (1 - odd), 16), 48), :] = blank
        wbuf[p, pl.ds(foff, 16), :] = up
        for lo in (0, 464):
            wa[p, lo:lo + 48, :] = blank[:, :ASPLIT]
            wb[p, lo:lo + 48, :] = blank[:, ASPLIT:]

    bar = pltpu.get_barrier_semaphore()
    for d in range(1, 8):
        pl.semaphore_signal(bar, inc=1, device_id={"tok": (t + d) % 8}, device_id_type=MESH)
    for idx in (hx(1), hx(-1), hy(1), hy(-1)):
        pl.semaphore_signal(bar, inc=1, device_id={"head": idx}, device_id_type=MESH)

    for r in range(4):
        loads[r].wait()

        def sq(kk, acc, r=r):
            blk = stream_v[pl.ds(64 * r, 64), pl.ds(pl.multiple_of(1024 * kk, 1024), 1024)].astype(F32)
            blk = blk * blk
            for b in range(8):
                acc = acc + blk[:, 128 * b:128 * b + 128]
            return acc

        acc = lax.fori_loop(0, 7, sq, jnp.zeros((64, 128), F32))
        mean = jnp.sum(acc, axis=1, keepdims=True) * (1.0 / WIDTH)
        rstd_v[pl.ds(64 * r, 64), :] = jnp.broadcast_to(lax.rsqrt(mean + 1e-5), (64, 128))
    pl.semaphore_wait(bar, 11)
    w_c.wait()
    for p in range(3):
        src = wbuf.at[p, sent, pl.ds(0, ASPLIT)]
        send(src, wa.at[p, sent], p_s.at[p, 0], p_r.at[p, 0], "head", dev_a)
        src = wbuf.at[p, sent, pl.ds(ASPLIT, COLS - ASPLIT)]
        send(src, wb.at[p, sent], p_s.at[p, 1], p_r.at[p, 1], "head", dev_b)
    kv_c.start()
    adown_c.wait()
    low_acc[...] = jnp.zeros((ROWS, RANK), F32)

    def low_step(kk, carry):
        parts = []
        for b in range(8):
            block = 8 * kk + b
            here = pl.ds(pl.multiple_of(128 * block, 128), 128)
            xb = stream_v[:, here].astype(F32)
            xn = (xb * rstd_v[...] * gain32[pl.ds(block, 1), :]).astype(BF16)
            stream_v[:, here] = xn
            parts.append(xn)
        low_acc[...] += mm(
            jnp.concatenate(parts, axis=1), adown_v[pl.ds(pl.multiple_of(1024 * kk, 1024), 1024), :]
        )
        return carry

    lax.fori_loop(0, 7, low_step, 0)
    low = low_acc[...].astype(BF16)

    def window(g):
        here = pl.ds(pl.multiple_of(128 * ((7 * g) // 2), 128), KW)
        spot = 448 - 400 * (g % 2)
        li = iota((RANK, KW), 1) - spot
        place = one((iota((RANK, KW), 0) - 8 * g == li) & (li >= 0) & (li < 8))
        terms = mm(low, place)
        lane = iota((ROWS, KW), 1) - 448 * (1 - g % 2)
        return jnp.where((lane >= 0) & (lane < 64), terms, stream_v[:, here].astype(F32)).astype(BF16)

    def rows_for(core_to, mine, dst):
        parity = jnp.where(core_to == 0, y % 2, x % 2)
        i = iota((128, ROWS), 0)
        i2, i1 = parity + 2 * (i // 64), (i // 16) % 4
        rank = 16 * jnp.where(core_to == 0, 4 * i2 + i1, 4 * i1 + i2) + i % 16
        pick = one(rank.astype(F32) == jnp.broadcast_to(rank_row, (128, ROWS)))
        step_a = 1 - 2 * parity
        for n, block in enumerate((None, step_a, -step_a)):
            if block is None:
                win = mine
            else:
                win = window(jnp.where(core_to == 0, ((y + block + 4) % 4) * 4 + x, y * 4 + (x + block + 4) % 4))
            dst[:, KW * n:KW * n + KW] = mm(pick, win).astype(BF16)

    mine_win = window(h)
    rows_for(1 - core, mine_win, pack)
    send(pack, xbuf.at[0, core], x_s.at[2], x_r.at[0], "tok", tz(0, True))
    rows_for(core, mine_win, xbuf.at[0, core])

    def x_send(src, to, si, ri, d):
        send(src, to, x_s.at[si], x_r.at[ri], "tok", tz(d))

    x_send(xbuf.at[0, core], xbuf.at[1, 0], 0, 1, 1)
    x_send(xbuf.at[0, core], xbuf.at[1, 1], 1, 2, -1)

    def x_mate():
        got = xbuf.at[0, 1 - core]
        wait(got, x_r.at[0])
        x_send(got, xbuf.at[2, 0], 3, 3, 1)
        x_send(got, xbuf.at[2, 1], 4, 4, -1)

    def x_relay(k):
        lo, hi = pl.ds(0, 64), pl.ds(64, 64)
        wait(xbuf.at[k, 0], x_r.at[2 * k - 1])
        x_send(xbuf.at[k, 0, lo], xbuf.at[3, k - 1, lo], 2 * k + 3, k + 4, 1)
        wait(xbuf.at[k, 1], x_r.at[2 * k])
        x_send(xbuf.at[k, 1, hi], xbuf.at[3, k - 1, hi], 2 * k + 4, k + 4, -1)

    def ag_own(buf, ss, rr):
        own = buf.at[t]
        send(own, own, ss.at[0], rr.at[1], "tok", tz(1))
        send(own, own, ss.at[1], rr.at[2], "tok", tz(-1))
        send(own, own, ss.at[2], rr.at[0], "tok", tz(0, True))

    def ag_near(buf, ss, rr, half):
        a, b = tz(-1), tz(1)
        wait(buf.at[a], rr.at[1])
        piece = buf.at[a, pl.ds(0, half)]
        send(piece, piece, ss.at[3], rr.at[3], "tok", tz(1))
        send(buf.at[a], buf.at[a], ss.at[4], rr.at[4], "tok", tz(0, True))
        wait(buf.at[b], rr.at[2])
        piece = buf.at[b, pl.ds(half, half)]
        send(piece, piece, ss.at[5], rr.at[3], "tok", tz(-1))
        send(buf.at[b], buf.at[b], ss.at[6], rr.at[5], "tok", tz(0, True))

    def ag_far(buf, ss, rr):
        c = tz(2)
        wait(buf.at[c], rr.at[3])
        send(buf.at[c], buf.at[c], ss.at[7], rr.at[6], "tok", tz(0, True))

    def ag_drain(buf, ss, half):
        for i in (0, 1, 2):
            wait(buf.at[t], ss.at[i])
        wait(buf.at[t, pl.ds(0, half)], ss.at[3])
        wait(buf.at[t], ss.at[4])
        wait(buf.at[t, pl.ds(0, half)], ss.at[5])
        wait(buf.at[t], ss.at[6])
        wait(buf.at[t], ss.at[7])

    def add2(a, b):
        return a.astype(F32) + b.astype(F32)

    def s_matmul(u):
        k, p = u // 3, u % 3
        base = mm(xbuf[k, :, :, 0:KW].reshape(256, KW), wbuf[p])
        a = base[:, :ASPLIT] + mm(xbuf[k, :, :, KW:2 * KW].reshape(256, KW), wa[p])
        part[u, :, :, :, :, 0:ASPLIT] = a.astype(BF16).reshape(2, 2, 4, 16, ASPLIT)
        b = base[:, ASPLIT:] + mm(xbuf[k, :, :, 2 * KW:3 * KW].reshape(256, KW), wb[p])
        part[u, :, :, :, :, ASPLIT:COLS] = b.astype(BF16).reshape(2, 2, 4, 16, COLS - ASPLIT)
        ss, rr = rs_s.at[0, u], rs_r.at[0, u]
        send(part.at[u, 0, :, cf], ra.at[u, 0], ss, rr, "head", dev1(1))
        send(part.at[u, 1, :, cf], ra.at[u, 1], ss, rr, "head", dev1(-1))

    def s_b1(u):
        wait(ra.at[u], rs_r.at[0, u])
        ss, rr = rs_s.at[1, u], rs_r.at[1, u]
        part[u, 0, :, cp] = add2(part[u, 0, :, cp], ra[u, 0]).astype(BF16)
        send(part.at[u, :, :, cp], rb.at[u, 0], ss, rr, "head", dev1(1))
        part[u, 1, :, cm] = add2(part[u, 1, :, cm], ra[u, 1]).astype(BF16)
        send(part.at[u, :, :, cm], rb.at[u, 1], ss, rr, "head", dev1(-1))

    def s_a2(u):
        wait(rb.at[u], rs_r.at[1, u])
        ss, rr = rs_s.at[2, u], rs_r.at[2, u]
        part[u, :, :, c1] = (add2(part[u, :, :, c1], rb[u, 0]) + rb[u, 1].astype(F32)).astype(BF16)
        send(part.at[u, 0, far_v, c1], rc.at[u, 0], ss, rr, "head", dev2(1))
        send(part.at[u, 1, far_v, c1], rc.at[u, 1], ss, rr, "head", dev2(-1))

    def s_b2(u):
        wait(rc.at[u], rs_r.at[2, u])
        ss, rr = rs_s.at[3, u], rs_r.at[3, u]
        send(rc.at[u, 0], rd.at[u, 0], ss, rr, "head", dev2(1))
        send(rc.at[u, 1], rd.at[u, 1], ss, rr, "head", dev2(-1))

    def s_fin(u):
        wait(rd.at[u], rs_r.at[3, u])
        k, p = u // 3, u % 3
        for e in range(2):
            qkv[p, 2 * k + e] = add2(part[u, e, own_v, c1], rd[u, e]).astype(BF16)

    def prepare():
        node_col = iota((128, 128), 0).astype(F32) + (128 * h).astype(F32)
        acc = jnp.zeros((128, 128), F32)
        for b in range(16):
            line = jnp.broadcast_to(nodes[b:b + 1, :].astype(F32), (128, 128))
            acc = acc + jnp.where(line == node_col, slot_of(b // 2).astype(F32), 0.0)
        slot_col = jnp.sum(acc, axis=1, keepdims=True)
        slot_row = row_of(slot_col)
        before = (jnp.broadcast_to(slot_col, (128, 128)) == jnp.broadcast_to(slot_row, (128, 128))) & (
            iota((128, 128), 1) < iota((128, 128), 0)
        )
        pos_col = 16.0 * slot_col + jnp.sum(jnp.where(before, 1.0, 0.0), axis=1, keepdims=True)
        pos_row = row_of(pos_col)
        node_qt[...] = one(iota((128, 128), 1).astype(F32) == jnp.broadcast_to(pos_col, (128, 128)))
        node_q[...] = one(iota((128, 128), 0).astype(F32) == jnp.broadcast_to(pos_row, (128, 128)))
        for r in range(2):
            up = column_of(parents[r:r + 1, :].astype(F32))
            i0, i1 = iota((NODES, NODES), 0), iota((NODES, NODES), 1)
            anc = one((i0 == i1) | (i1.astype(F32) == jnp.broadcast_to(up, (NODES, NODES))))
            for _ in range(6):
                anc = jnp.minimum(mm(anc, anc), 1.0).astype(BF16)
            anc_v[r] = anc.astype(F32)
        m_v[...] = jnp.full(m_v.shape, NEG, F32)
        l_v[...] = jnp.zeros(l_v.shape, F32)
        acc_v[...] = jnp.zeros(acc_v.shape, F32)

    def in_nodes(p):
        return mm(node_qt[...], qkv[p].reshape(128, COLS))

    def spread_queries():
        q = in_nodes(0)
        head_of = iota((NODES, COLS), 1) // HEAD
        for r in range(2):
            qr = q[NODES * r:NODES * r + NODES]
            for j in range(LOCAL_HEADS):
                qbd[r, NODES * j:NODES * j + NODES, :] = jnp.where(head_of == j, qr, 0.0).astype(BF16)

    scale = HEAD ** -0.5

    def soften(r, s, values):
        m_old = m_v[r]
        m_new = jnp.maximum(m_old, jnp.broadcast_to(jnp.max(s, axis=1, keepdims=True), m_old.shape))
        shrink = jnp.exp(m_old - m_new)
        e = jnp.exp(s - m_new[:, 0:1])
        m_v[r] = m_new
        l_v[r] = l_v[r] * shrink + jnp.broadcast_to(jnp.sum(e, axis=1, keepdims=True), m_old.shape)
        acc_v[r] = acc_v[r] * shrink[:, 0:1] + mm(e.astype(BF16), values)

    def cache_piece(i):
        r, c = i // 4, i % 4
        here = pl.ds(pl.multiple_of(PIECE * c, PIECE), PIECE)
        s = lax.dot_general(qbd[r], kv_v[0, r, here, :], NT, preferred_element_type=F32) * scale
        live = iota((256, PIECE), 1) + PIECE * c < clen[r]
        soften(r, jnp.where(live, s, NEG), kv_v[1, r, here, :])

    start_att = 9 + 4 * LAG
    last = start_att + 8

    def body(it, carry):
        for lag, stage in ((4 * LAG, s_fin), (3 * LAG, s_b2), (2 * LAG, s_a2), (LAG, s_b1)):
            @pl.when((it >= lag) & (it < UNITS + lag))
            def _(lag=lag, stage=stage):
                stage(it - lag)

        @pl.when(it < UNITS)
        def _():
            @pl.when(it < 3)
            def _():
                wait(wa.at[it, sent], p_r.at[it, 0])
                wait(wb.at[it, sent], p_r.at[it, 1])

            @pl.when(it == 0)
            def _():
                x_mate()

            @pl.when(it == 3)
            def _():
                x_relay(1)

            @pl.when(it == 6)
            def _():
                x_relay(2)

            @pl.when(it == 9)
            def _():
                wait(xbuf.at[3, 0], x_r.at[5])
                wait(xbuf.at[3, 1], x_r.at[6])

            s_matmul(it)

        @pl.when(it == 1)
        def _():
            prepare()

        @pl.when(it == 6)
        def _():
            wo_c.wait()
            ag_own(wo_v, w_s, w_r)

        @pl.when(it == 11)
        def _():
            ag_near(wo_v, w_s, w_r, HEAD // 2)

        @pl.when(it == start_att + 5)
        def _():
            ag_far(wo_v, w_s, w_r)

        @pl.when(it == start_att)
        def _():
            kv_c.wait()
            spread_queries()

        @pl.when((it >= start_att) & (it < start_att + 8))
        def _():
            cache_piece(it - start_att)

        return carry

    lax.fori_loop(0, last, body, 0)

    def drain_rs():
        for i in (0, 1, 3, 4):
            wait(xbuf.at[0, 0], x_s.at[i])
        wait(pack, x_s.at[2])
        for i in (5, 6, 7, 8):
            wait(xbuf.at[0, 0, pl.ds(0, 64)], x_s.at[i])
        ag_drain(wo_v, w_s, HEAD // 2)
        for i, c in ((0, tz(0, True)), (4, tz(-1, True)), (5, tz(1, True)), (6, tz(2, True))):
            wait(wo_v.at[c], w_r.at[i])
        for p in range(3):
            wait(wa.at[p, sent], p_s.at[p, 0])
            wait(wb.at[p, sent], p_s.at[p, 1])

        def drain(u, carry):
            for k, ref in enumerate((ra, rb, rc, rd)):
                wait(ref.at[u], rs_s.at[k, u])
            return carry

        lax.fori_loop(0, UNITS, drain, 0)


    k_n, v_n = in_nodes(1).astype(BF16), in_nodes(2).astype(BF16)
    outs = []
    for r in range(2):
        rows = slice(NODES * r, NODES * r + NODES)
        s = lax.dot_general(qbd[r], k_n[rows], NT, preferred_element_type=F32) * scale
        keep = jnp.concatenate([anc_v[r]] * LOCAL_HEADS, axis=0) > 0.5
        soften(r, jnp.where(keep, s, NEG), v_n[rows])
        norm = acc_v[r] / l_v[r][:, 0:1]
        head_of = iota((NODES, COLS), 1) // HEAD
        o = jnp.zeros((NODES, COLS), F32)
        for j in range(LOCAL_HEADS):
            o = jnp.where(head_of == j, norm[NODES * j:NODES * j + NODES], o)
        outs.append(o.astype(BF16))
    att[...] = mm(node_q[...], jnp.concatenate(outs, axis=0)).astype(BF16).reshape(8, 16, COLS)

    for d in range(1, 8):
        to = (t + d) % 8
        send(att.at[slot_of(to)], res.at[t, h], aa_s.at[d - 1], aa_r.at[d - 1], "tok", to)
    res[t, h] = att[core]
    for r in range(2):
        col = column_of(accepted[r:r + 1, :].astype(F32)) + float(NODES * r)
        pick = one(iota((8, 128), 1).astype(F32) == jnp.broadcast_to(col, (8, 128)))
        akv_ref[0, r] = mm(pick, k_n).astype(BF16)
        akv_ref[1, r] = mm(pick, v_n).astype(BF16)
    for d in range(1, 8):
        wait(res.at[(t - d + 8) % 8, h], aa_r.at[d - 1])


    steps = (0, -1, 1, 2)

    def slot(hf, i, j):
        if hf == 0:
            return ((y + j + 4) % 4) * 4 + (x + i + 4) % 4
        return ((y + i + 4) % 4) * 4 + (x + j + 4) % 4

    def blk(hf, i, j, part_of=None):
        lo, n = (4 * hf, 4) if part_of is None else (4 * hf + 2 * part_of, 2)
        return res.at[pl.ds(lo, n), slot(hf, i, j)]

    def dev(hf, axis, d):
        return slot(hf, d, 0) if axis == 0 else slot(hf, 0, d)

    def first_sends(hf):
        for n, d in enumerate((1, -1)):
            send(blk(hf, 0, 0), blk(hf, 0, 0), g1_s.at[hf, n], g1_r.at[hf, n], "head", dev(hf, 0, d))

    def cross_sends(hf, n_i):
        i = steps[n_i]
        for n, d in enumerate((1, -1)):
            send(blk(hf, i, 0), blk(hf, i, 0), g3_s.at[hf, n_i, n], g3_r.at[hf, n_i, n], "head", dev(hf, 1, d))

    def cross_forward(hf, n_i):
        i = steps[n_i]
        for n, d in enumerate((1, -1)):
            wait(blk(hf, i, -d), g3_r.at[hf, n_i, n])
            send(blk(hf, i, -d, n), blk(hf, i, -d, n), g4_s.at[hf, n_i, n], g4_r.at[hf, n_i], "head", dev(hf, 1, d))

    for hf in range(2):
        first_sends(hf)
    for hf in range(2):
        cross_sends(hf, 0)
    for hf in range(2):
        for n, d in enumerate((1, -1)):
            wait(blk(hf, -d, 0), g1_r.at[hf, n])
            send(blk(hf, -d, 0, n), blk(hf, -d, 0, n), g2_s.at[hf, n], g2_r.at[hf], "head", dev(hf, 0, d))
            cross_sends(hf, 1 + n)
    for hf in range(2):
        cross_forward(hf, 0)
    for hf in range(2):
        wait(blk(hf, 2, 0), g2_r.at[hf])
        cross_sends(hf, 3)
    for n_i in (1, 2, 3):
        for hf in range(2):
            cross_forward(hf, n_i)

    drain_rs()
    for hf in range(2):
        for n_i in range(4):
            wait(blk(hf, steps[n_i], 2), g4_r.at[hf, n_i])

    total = jnp.zeros((HEAD, ROWS), F32)
    for s in range(8):
        total = total + lax.dot_general(
            wo_v[s], res[s].reshape(ROWS, COLS), NT, preferred_element_type=F32
        )
    out_ref[...] = mm(total.astype(BF16), sort_p[...]).astype(BF16)

    for d in range(1, 8):
        wait(att.at[0], aa_s.at[d - 1])
    for hf in range(2):
        for n in range(2):
            wait(blk(hf, 0, 0), g1_s.at[hf, n])
            wait(blk(hf, 0, 0, 0), g2_s.at[hf, n])
            for n_i in range(4):
                wait(blk(hf, 0, 0), g3_s.at[hf, n_i, n])
                wait(blk(hf, 0, 0, 0), g4_s.at[hf, n_i, n])


def on_device(stream, row_tree_nodes, gain, wqkv, adown, aup, kv, clen, parents, accepted, wo):
    vm = pl.BlockSpec(memory_space=pltpu.VMEM)
    hbm = pl.BlockSpec(memory_space=pl.ANY)
    sm = pl.BlockSpec(memory_space=pltpu.SMEM)
    dma = pltpu.SemaphoreType.DMA
    v = pltpu.VMEM
    out_t, akv = pl.pallas_call(
        kernel,
        out_shape=(
            jax.ShapeDtypeStruct((HEAD, ROWS), BF16),
            jax.ShapeDtypeStruct((2, 2, 8, COLS), BF16),
        ),
        in_specs=[hbm, vm, vm, hbm, hbm, vm, hbm, sm, vm, vm, hbm],
        out_specs=(vm, vm),
        scratch_shapes=[
            v((ROWS, WIDTH), BF16), v((56, 128), F32), v((WIDTH, RANK), BF16), v((ROWS, RANK), F32),
            v((ROWS, 128), F32), v((3, KW, COLS), BF16), v((3, KW, ASPLIT), BF16),
            v((3, KW, COLS - ASPLIT), BF16), v((2, 2, 2048, COLS), BF16), v((4, 2, 128, 3 * KW), BF16),
            v((128, 3 * KW), BF16),
            v((8, HEAD, COLS), BF16), v((UNITS, 2, 2, 4, 16, COLS), BF16),
            v((UNITS, 2, 2, 16, COLS), BF16), v((UNITS, 2, 2, 2, 16, COLS), BF16),
            v((UNITS, 2, 16, COLS), BF16), v((UNITS, 2, 16, COLS), BF16),
            v((3, 8, 16, COLS), BF16), v((ROWS, ROWS), BF16), v((128, 128), BF16), v((128, 128), BF16),
            v((2, NODES, NODES), F32), v((2, 256, COLS), BF16), v((2, 256, COLS), F32),
            v((2, 256, 128), F32), v((2, 256, 128), F32), v((8, 16, COLS), BF16), v((8, 16, 16, COLS), BF16),
            dma((8,)), dma((9,)), dma((7,)), dma((8,)), dma((7,)), dma((3, 2)), dma((3, 2)), dma((4, UNITS)), dma((4, UNITS)),
            dma((7,)), dma((7,)), dma((2, 2)), dma((2, 2)), dma((2, 2)), dma((2,)),
            dma((2, 4, 2)), dma((2, 4, 2)), dma((2, 4, 2)), dma((2, 4)),
        ],
        compiler_params=pltpu.CompilerParams(
            collective_id=0, has_side_effects=True, vmem_limit_bytes=67043328
        ),
        name="tree_verify",
    )(
        stream, row_tree_nodes.reshape(16, 128), gain.reshape(56, 128), jnp.transpose(wqkv, (1, 0, 2)),
        adown, jnp.transpose(aup, (1, 0, 2)), kv, clen, parents, accepted, jnp.transpose(wo),
    )
    return jnp.transpose(out_t), akv


def solution(mesh):
    placed = (
        P("tok", None), P(), P(), P("head", None, "tok"), P(), P("head", None, "tok"),
        P(None, "head", None, "tok"), P("head"), P("head", None), P("head", None), P("tok", "head"),
    )
    return jax.shard_map(
        on_device, mesh=mesh, in_specs=placed,
        out_specs=(P("tok", "head"), P(None, "head", None, "tok")), check_vma=False,
    )
```

```python
import functools

import jax
import jax.numpy as jnp
from jax import lax
from jax.experimental import pallas as pl
from jax.experimental.pallas import tpu as pltpu
from jax.sharding import PartitionSpec as P

MESH = pl.DeviceIdType.MESH
F32 = jnp.float32
BF16 = jnp.bfloat16

WIDTH = 7168
COLS = 896
HEAD = 224
LOCAL_HEADS = 4
RANK = 128
NODES = 64
ROWS = 256
KW = 512
UNITS = 12
LAG = 3
ASPLIT = 512
SENT = 464
PIECE = 512
NEG = float("-inf")
NT = (((1,), (1,)), ((), ()))


def iota(shape, dim):
    return lax.broadcasted_iota(jnp.int32, shape, dim)


def mm(a, b):
    return jnp.dot(a, b, preferred_element_type=F32)


def column_of(row):
    n = row.shape[1]
    eye = iota((n, n), 0) == iota((n, n), 1)
    return jnp.sum(jnp.where(eye, jnp.broadcast_to(row, (n, n)), 0.0), axis=1, keepdims=True)


def row_of(col):
    n = col.shape[0]
    eye = iota((n, n), 0) == iota((n, n), 1)
    return jnp.sum(jnp.where(eye, jnp.broadcast_to(col, (n, n)), 0.0), axis=0, keepdims=True)


def one(mask):
    return jnp.where(mask, 1.0, 0.0).astype(BF16)


def kernel(
    stream_h, nodes, gain, wqkv_h, adown_h, aup, kv_h, clen, parents, accepted, wo_h,
    out_ref, akv_ref,
    stream_v, gain32, adown_v, low_acc, rstd_v, wbuf, wa, wb, kv_v, xbuf, pack, wo_v, part,
    ra, rb, mine_sum, qkv, sort_p, node_q, node_qt, anc_v, qbd, acc_v, m_v, l_v, att, res,
    ld, x_s, x_r, w_s, w_r, p_s, p_r, rs_s, rs_r, aa_s, aa_r, g1_s, g1_r, g2_s, g2_r, g3_s, g3_r, g4_s, g4_r,
):
    t = lax.axis_index("tok")
    h = lax.axis_index("head")
    z, core = t // 2, t % 2
    y, x = h // 4, h % 4

    def hx(d):
        return y * 4 + (x + d + 4) % 4

    def hy(d):
        return ((y + d + 4) % 4) * 4 + x

    c1, c2 = jnp.where(core == 0, x, y), jnp.where(core == 0, y, x)
    par = c2 % 2

    def dev1(d):
        return jnp.where(core == 0, hx(d), hy(d))

    def dev2(d):
        return jnp.where(core == 0, hy(d), hx(d))

    dev_a = jnp.where(par == 0, dev2(1), dev2(-1))
    dev_b = jnp.where(par == 0, dev2(-1), dev2(1))

    def tz(d, other=False):
        c = 1 - core if other else core
        return ((z + d + 4) % 4) * 2 + c

    cm, cp, cf = (c1 + 3) % 4, (c1 + 1) % 4, (c1 + 2) % 4
    own_v = c2 // 2
    far_v = 1 - own_v

    def slot_of(tok):
        dz, same = (tok // 2 - z + 4) % 4, tok % 2 == core
        near = jnp.where(same, 2, 4) + jnp.where(dz == 1, 1, 0)
        far = jnp.where(same, 6, 7)
        return jnp.where(dz == 0, tok % 2, jnp.where(dz == 2, far, near))

    def send(src, dst, ssem, rsem, axis, idx):
        pltpu.make_async_remote_copy(
            src_ref=src, dst_ref=dst, send_sem=ssem, recv_sem=rsem,
            device_id={axis: idx}, device_id_type=MESH,
        ).start()

    def wait(ref, sem):
        pltpu.make_async_copy(ref, ref, sem).wait()

    odd = h % 2
    koff = pl.multiple_of(64 * odd, 64)
    foff = pl.multiple_of(448 - 400 * odd, 16)
    sent = pl.ds(pl.multiple_of(48 * odd, 16), SENT)
    w_c = pltpu.make_async_copy(wqkv_h, wbuf.at[:, pl.ds(koff, 448), :], ld.at[5])
    w_c.start()
    loads = []
    for r in range(4):
        c = pltpu.make_async_copy(
            stream_h.at[pl.ds(64 * r, 64)], stream_v.at[pl.ds(64 * r, 64)], ld.at[r]
        )
        c.start()
        loads.append(c)
    adown_c = pltpu.make_async_copy(adown_h, adown_v, ld.at[4])
    adown_c.start()
    wo_c = pltpu.make_async_copy(wo_h, wo_v.at[t], ld.at[6])
    wo_c.start()
    kv_c = pltpu.make_async_copy(kv_h, kv_v, ld.at[7])

    blank = jnp.zeros((48, COLS), BF16)
    for p in range(3):
        for lo in (0, 464):
            wa[p, lo:lo + 48, :] = blank[:, :ASPLIT]
            wb[p, lo:lo + 48, :] = blank[:, ASPLIT:]

    bar = pltpu.get_barrier_semaphore()
    for d in range(1, 8):
        pl.semaphore_signal(bar, inc=1, device_id={"tok": (t + d) % 8}, device_id_type=MESH)
    for idx in (hx(1), hx(-1), hx(2), hy(1), hy(-1), hy(2)):
        pl.semaphore_signal(bar, inc=1, device_id={"head": idx}, device_id_type=MESH)

    for p in range(3):
        up = jnp.concatenate([aup[p].astype(F32), jnp.zeros((8, COLS), F32)], axis=0).astype(BF16)
        wbuf[p, pl.ds(pl.multiple_of(464 * (1 - odd), 16), 48), :] = blank
        wbuf[p, pl.ds(foff, 16), :] = up

    mine = nodes[pl.ds(2 * t, 2), :].astype(F32)
    key_row = jnp.concatenate([mine[0:1], mine[1:2]], axis=1)
    key_col = column_of(key_row)
    rank_row = jnp.sum(
        jnp.where(
            jnp.broadcast_to(key_col, (ROWS, ROWS)) < jnp.broadcast_to(key_row, (ROWS, ROWS)), 1.0, 0.0
        ),
        axis=0, keepdims=True,
    )
    sort_p[...] = one(iota((ROWS, ROWS), 0).astype(F32) == jnp.broadcast_to(rank_row, (ROWS, ROWS)))
    gain32[...] = gain[...].astype(F32)

    def finish_cut():
        for c in (wo_c, kv_c):
            c.wait()
        for p in range(3):
            wait(wa.at[p, sent], p_r.at[p, 0])
            wait(wb.at[p, sent], p_r.at[p, 1])
            wait(wa.at[p, sent], p_s.at[p, 0])
            wait(wb.at[p, sent], p_s.at[p, 1])
        out_ref[...] = jnp.zeros(out_ref.shape, BF16)
        akv_ref[...] = jnp.zeros(akv_ref.shape, BF16)

    for r in range(4):
        loads[r].wait()

        def sq(kk, acc, r=r):
            blk = stream_v[pl.ds(64 * r, 64), pl.ds(pl.multiple_of(1024 * kk, 1024), 1024)].astype(F32)
            blk = blk * blk
            for b in range(8):
                acc = acc + blk[:, 128 * b:128 * b + 128]
            return acc

        acc = lax.fori_loop(0, 7, sq, jnp.zeros((64, 128), F32))
        mean = jnp.sum(acc, axis=1, keepdims=True) * (1.0 / WIDTH)
        rstd_v[pl.ds(64 * r, 64), :] = jnp.broadcast_to(lax.rsqrt(mean + 1e-5), (64, 128))
    pl.semaphore_wait(bar, 13)
    w_c.wait()
    for p in range(3):
        src = wbuf.at[p, sent, pl.ds(0, ASPLIT)]
        send(src, wa.at[p, sent], p_s.at[p, 0], p_r.at[p, 0], "head", dev_a)
        src = wbuf.at[p, sent, pl.ds(ASPLIT, COLS - ASPLIT)]
        send(src, wb.at[p, sent], p_s.at[p, 1], p_r.at[p, 1], "head", dev_b)

    kv_c.start()
    adown_c.wait()
    low_acc[...] = jnp.zeros((ROWS, RANK), F32)

    def low_step(kk, carry):
        parts = []
        for b in range(8):
            block = 8 * kk + b
            here = pl.ds(pl.multiple_of(128 * block, 128), 128)
            xb = stream_v[:, here].astype(F32)
            xn = (xb * rstd_v[...] * gain32[pl.ds(block, 1), :]).astype(BF16)
            stream_v[:, here] = xn
            parts.append(xn)
        low_acc[...] += mm(
            jnp.concatenate(parts, axis=1), adown_v[pl.ds(pl.multiple_of(1024 * kk, 1024), 1024), :]
        )
        return carry

    lax.fori_loop(0, 7, low_step, 0)
    low = low_acc[...].astype(BF16)

    def window(g):
        here = pl.ds(pl.multiple_of(128 * ((7 * g) // 2), 128), KW)
        spot = 448 - 400 * (g % 2)
        li = iota((RANK, KW), 1) - spot
        place = one((iota((RANK, KW), 0) - 8 * g == li) & (li >= 0) & (li < 8))
        terms = mm(low, place)
        lane = iota((ROWS, KW), 1) - 448 * (1 - g % 2)
        return jnp.where((lane >= 0) & (lane < 64), terms, stream_v[:, here].astype(F32)).astype(BF16)

    def rows_for(core_to, mine, dst):
        parity = jnp.where(core_to == 0, y % 2, x % 2)
        i = iota((128, ROWS), 0)
        i2, i1 = parity + 2 * (i // 64), (i // 16) % 4
        rank = 16 * jnp.where(core_to == 0, 4 * i2 + i1, 4 * i1 + i2) + i % 16
        pick = one(rank.astype(F32) == jnp.broadcast_to(rank_row, (128, ROWS)))
        step_a = 1 - 2 * parity
        for n, block in enumerate((None, step_a, -step_a)):
            if block is None:
                win = mine
            else:
                win = window(jnp.where(core_to == 0, ((y + block + 4) % 4) * 4 + x, y * 4 + (x + block + 4) % 4))
            dst[:, KW * n:KW * n + KW] = mm(pick, win).astype(BF16)

    mine_win = window(h)
    def x_send(src, to, si, ri, d):
        send(src, to, x_s.at[si], x_r.at[ri], "tok", tz(d))

    rows_for(core, mine_win, xbuf.at[0, core])
    x_send(xbuf.at[0, core], xbuf.at[1, 0], 0, 1, 1)
    x_send(xbuf.at[0, core], xbuf.at[1, 1], 1, 2, -1)
    rows_for(1 - core, mine_win, pack)
    send(pack, xbuf.at[0, core], x_s.at[2], x_r.at[0], "tok", tz(0, True))

    def x_mate():
        got = xbuf.at[0, 1 - core]
        wait(got, x_r.at[0])
        x_send(got, xbuf.at[2, 0], 3, 3, 1)
        x_send(got, xbuf.at[2, 1], 4, 4, -1)

    def x_relay(k):
        lo, hi = pl.ds(0, 64), pl.ds(64, 64)
        x_send(xbuf.at[k, 0, lo], xbuf.at[3, k - 1, lo], 3 + 2 * k, k + 4, 1)
        x_send(xbuf.at[k, 1, hi], xbuf.at[3, k - 1, hi], 4 + 2 * k, k + 4, -1)

    near = tuple((d, tz(d)) for d in (-1, 1, 2))

    def wo_own():
        own = wo_v.at[t]
        send(own, own, w_s.at[0], w_r.at[0], "tok", tz(0, True))
        for n, d in enumerate((1, -1, 2)):
            send(own, own, w_s.at[1 + n], w_r.at[1 + n], "tok", tz(d))

    def wo_mate():
        for n, (d, src) in enumerate(near):
            wait(wo_v.at[src], w_r.at[1 + n])
            send(wo_v.at[src], wo_v.at[src], w_s.at[4 + n], w_r.at[4 + n], "tok", tz(0, True))

    def wo_rest():
        wait(wo_v.at[t], w_r.at[0])
        for n in range(3):
            wait(wo_v.at[t], w_r.at[4 + n])
        for n in range(7):
            wait(wo_v.at[t], w_s.at[n])

    def add2(a, b):
        return a.astype(F32) + b.astype(F32)

    def s_matmul(u):
        k, p = u // 3, u % 3
        base = mm(xbuf[k, :, :, 0:KW].reshape(256, KW), wbuf[p])
        a = base[:, :ASPLIT] + mm(xbuf[k, :, :, KW:2 * KW].reshape(256, KW), wa[p])
        part[u, :, :, :, :, 0:ASPLIT] = a.astype(BF16).reshape(2, 2, 4, 16, ASPLIT)
        b = base[:, ASPLIT:] + mm(xbuf[k, :, :, 2 * KW:3 * KW].reshape(256, KW), wb[p])
        part[u, :, :, :, :, ASPLIT:COLS] = b.astype(BF16).reshape(2, 2, 4, 16, COLS - ASPLIT)
        s_a1(u)

    def s_a1(u):
        ss, rr = rs_s.at[0, u], rs_r.at[0, u]
        send(part.at[u, 0, :, cf], ra.at[u, 2, 0], ss, rr, "head", dev1(1))
        send(part.at[u, 1, :, cf], ra.at[u, 2, 1], ss, rr, "head", dev1(-1))

    def s_b1(u):
        wait(ra.at[u, 2], rs_r.at[0, u])
        ss, rr = rs_s.at[2, u], rs_r.at[2, u]
        part[u, 0, :, cp] = add2(part[u, 0, :, cp], ra[u, 2, 0]).astype(BF16)
        send(part.at[u, :, :, cp], ra.at[u, 0], ss, rr, "head", dev1(1))
        part[u, 1, :, cm] = add2(part[u, 1, :, cm], ra[u, 2, 1]).astype(BF16)
        send(part.at[u, :, :, cm], ra.at[u, 1], ss, rr, "head", dev1(-1))

    def s_sum(u):
        wait(ra.at[u, 0:2], rs_r.at[2, u])
        ss, rr = rs_s.at[1, u], rs_r.at[1, u]

        def total(v):
            a = add2(part[u, :, v, c1], ra[u, 0, :, v])
            return a + ra[u, 1, :, v].astype(F32)
            return a + add2(ra[u, 1, :, v], ra[u, 2, :, v])

        part[u, :, far_v, c1] = total(far_v).astype(BF16)
        send(part.at[u, :, far_v, c1], rb.at[u], ss, rr, "head", dev2(2))
        mine_sum[u] = total(own_v)

    def s_fin(u):
        wait(rb.at[u], rs_r.at[1, u])
        k, p = u // 3, u % 3
        for e in range(2):
            qkv[p, 2 * k + e] = (mine_sum[u, e] + rb[u, e].astype(F32)).astype(BF16)

    def prepare():
        node_col = iota((128, 128), 0).astype(F32) + (128 * h).astype(F32)
        acc = jnp.zeros((128, 128), F32)
        for b in range(16):
            line = jnp.broadcast_to(nodes[b:b + 1, :].astype(F32), (128, 128))
            acc = acc + jnp.where(line == node_col, slot_of(b // 2).astype(F32), 0.0)
        slot_col = jnp.sum(acc, axis=1, keepdims=True)
        slot_row = row_of(slot_col)
        before = (jnp.broadcast_to(slot_col, (128, 128)) == jnp.broadcast_to(slot_row, (128, 128))) & (
            iota((128, 128), 1) < iota((128, 128), 0)
        )
        pos_col = 16.0 * slot_col + jnp.sum(jnp.where(before, 1.0, 0.0), axis=1, keepdims=True)
        pos_row = row_of(pos_col)
        node_qt[...] = one(iota((128, 128), 1).astype(F32) == jnp.broadcast_to(pos_col, (128, 128)))
        node_q[...] = one(iota((128, 128), 0).astype(F32) == jnp.broadcast_to(pos_row, (128, 128)))
        for r in range(2):
            up = column_of(parents[r:r + 1, :].astype(F32))
            i0, i1 = iota((NODES, NODES), 0), iota((NODES, NODES), 1)
            anc = one((i0 == i1) | (i1.astype(F32) == jnp.broadcast_to(up, (NODES, NODES))))
            for _ in range(6):
                anc = jnp.minimum(mm(anc, anc), 1.0).astype(BF16)
            anc_v[r] = anc.astype(F32)
        m_v[...] = jnp.full(m_v.shape, NEG, F32)
        l_v[...] = jnp.zeros(l_v.shape, F32)
        acc_v[...] = jnp.zeros(acc_v.shape, F32)

    def in_nodes(p):
        return mm(node_qt[...], qkv[p].reshape(128, COLS))

    def spread_queries():
        q = in_nodes(0)
        head_of = iota((NODES, COLS), 1) // HEAD
        for r in range(2):
            qr = q[NODES * r:NODES * r + NODES]
            for j in range(LOCAL_HEADS):
                qbd[r, NODES * j:NODES * j + NODES, :] = jnp.where(head_of == j, qr, 0.0).astype(BF16)

    scale = HEAD ** -0.5

    def soften(r, s, values):
        m_old = m_v[r]
        m_new = jnp.maximum(m_old, jnp.broadcast_to(jnp.max(s, axis=1, keepdims=True), m_old.shape))
        shrink = jnp.exp(m_old - m_new)
        e = jnp.exp(s - m_new[:, 0:1])
        m_v[r] = m_new
        l_v[r] = l_v[r] * shrink + jnp.broadcast_to(jnp.sum(e, axis=1, keepdims=True), m_old.shape)
        acc_v[r] = acc_v[r] * shrink[:, 0:1] + mm(e.astype(BF16), values)

    def cache_piece(i):
        r, c = i // 4, i % 4
        here = pl.ds(pl.multiple_of(PIECE * c, PIECE), PIECE)
        s = lax.dot_general(qbd[r], kv_v[0, r, here, :], NT, preferred_element_type=F32) * scale
        live = iota((256, PIECE), 1) + PIECE * c < clen[r]
        soften(r, jnp.where(live, s, NEG), kv_v[1, r, here, :])

    start_att = 9 + (3) * LAG
    last = start_att + 8

    def body(it, carry):
        stages = ((3 * LAG, s_fin), (2 * LAG, s_sum), (LAG, s_b1))
        for lag, stage in stages:
            @pl.when((it >= lag) & (it < UNITS + lag))
            def _(lag=lag, stage=stage):
                stage(it - lag)

        @pl.when(it < UNITS)
        def _():
            @pl.when(it < 3)
            def _():
                wait(wa.at[it, sent], p_r.at[it, 0])
                wait(wb.at[it, sent], p_r.at[it, 1])

            @pl.when(it == 0)
            def _():
                x_mate()

            @pl.when((it == 3) | (it == 6) | (it == 9))
            def _():
                k = it // 3
                wait(xbuf.at[k, 0], x_r.at[2 * k - 1])
                wait(xbuf.at[k, 1], x_r.at[2 * k])
                @pl.when(it < 9)
                def _():
                    x_relay(k)

            s_matmul(it)

        @pl.when(it == 1)
        def _():
            prepare()

        @pl.when(it == 8)
        def _():
            wo_c.wait()
            wo_own()

        @pl.when(it == start_att + 4)
        def _():
            wo_mate()

        @pl.when(it == start_att)
        def _():
            kv_c.wait()
            spread_queries()

        @pl.when((it >= start_att) & (it < start_att + 8))
        def _():
            cache_piece(it - start_att)

        return carry

    lax.fori_loop(0, last, body, 0)

    def drain_rs():
        for i in range(5):
            wait(xbuf.at[0, 0], x_s.at[i])
        for i in range(5, 9):
            wait(xbuf.at[0, 0, pl.ds(0, 64)], x_s.at[i])
        wo_rest()
        for p in range(3):
            wait(wa.at[p, sent], p_s.at[p, 0])
            wait(wb.at[p, sent], p_s.at[p, 1])

        def drain(u, carry):
            for k, ref in enumerate((ra.at[:, 2], rb, ra.at[:, 0:2])):
                wait(ref.at[u], rs_s.at[k, u])
            return carry

        lax.fori_loop(0, UNITS, drain, 0)

    k_n, v_n = in_nodes(1).astype(BF16), in_nodes(2).astype(BF16)
    outs = []
    for r in range(2):
        rows = slice(NODES * r, NODES * r + NODES)
        s = lax.dot_general(qbd[r], k_n[rows], NT, preferred_element_type=F32) * scale
        keep = jnp.concatenate([anc_v[r]] * LOCAL_HEADS, axis=0) > 0.5
        soften(r, jnp.where(keep, s, NEG), v_n[rows])
        norm = acc_v[r] / l_v[r][:, 0:1]
        head_of = iota((NODES, COLS), 1) // HEAD
        o = jnp.zeros((NODES, COLS), F32)
        for j in range(LOCAL_HEADS):
            o = jnp.where(head_of == j, norm[NODES * j:NODES * j + NODES], o)
        outs.append(o.astype(BF16))
    att[...] = mm(node_q[...], jnp.concatenate(outs, axis=0)).astype(BF16).reshape(8, 16, COLS)

    for d in range(1, 8):
        to = (t + d) % 8
        send(att.at[slot_of(to)], res.at[t, h], aa_s.at[d - 1], aa_r.at[d - 1], "tok", to)
    res[t, h] = att[core]
    for r in range(2):
        col = column_of(accepted[r:r + 1, :].astype(F32)) + float(NODES * r)
        pick = one(iota((8, 128), 1).astype(F32) == jnp.broadcast_to(col, (8, 128)))
        akv_ref[0, r] = mm(pick, k_n).astype(BF16)
        akv_ref[1, r] = mm(pick, v_n).astype(BF16)
    for d in range(1, 8):
        wait(res.at[(t - d + 8) % 8, h], aa_r.at[d - 1])

    steps = (0, -1, 1, 2)

    def slot(hf, i, j):
        if hf == 0:
            return ((y + j + 4) % 4) * 4 + (x + i + 4) % 4
        return ((y + i + 4) % 4) * 4 + (x + j + 4) % 4

    def blk(hf, i, j, part_of=None):
        lo, n = (4 * hf, 4) if part_of is None else (4 * hf + 2 * part_of, 2)
        return res.at[pl.ds(lo, n), slot(hf, i, j)]

    def dev(hf, axis, d):
        return slot(hf, d, 0) if axis == 0 else slot(hf, 0, d)

    def first_sends(hf):
        for n, d in enumerate((1, -1)):
            send(blk(hf, 0, 0), blk(hf, 0, 0), g1_s.at[hf, n], g1_r.at[hf, n], "head", dev(hf, 0, d))

    def cross_sends(hf, n_i):
        i = steps[n_i]
        for n, d in enumerate((1, -1)):
            send(blk(hf, i, 0), blk(hf, i, 0), g3_s.at[hf, n_i, n], g3_r.at[hf, n_i, n], "head", dev(hf, 1, d))

    def cross_forward(hf, n_i):
        i = steps[n_i]
        for n, d in enumerate((1, -1)):
            wait(blk(hf, i, -d), g3_r.at[hf, n_i, n])
            send(blk(hf, i, -d, n), blk(hf, i, -d, n), g4_s.at[hf, n_i, n], g4_r.at[hf, n_i], "head", dev(hf, 1, d))

    for hf in range(2):
        first_sends(hf)
    for hf in range(2):
        cross_sends(hf, 0)
    for hf in range(2):
        for n, d in enumerate((1, -1)):
            wait(blk(hf, -d, 0), g1_r.at[hf, n])
            send(blk(hf, -d, 0, n), blk(hf, -d, 0, n), g2_s.at[hf, n], g2_r.at[hf], "head", dev(hf, 0, d))
            cross_sends(hf, 1 + n)
    for hf in range(2):
        cross_forward(hf, 0)
    for hf in range(2):
        wait(blk(hf, 2, 0), g2_r.at[hf])
        cross_sends(hf, 3)
    for n_i in (1, 2, 3):
        for hf in range(2):
            cross_forward(hf, n_i)

    drain_rs()
    for hf in range(2):
        for n_i in range(4):
            wait(blk(hf, steps[n_i], 2), g4_r.at[hf, n_i])

    total = jnp.zeros((HEAD, ROWS), F32)
    for s in range(8):
        total = total + lax.dot_general(
            wo_v[s], res[s].reshape(ROWS, COLS), NT, preferred_element_type=F32
        )
    out_ref[...] = mm(total.astype(BF16), sort_p[...]).astype(BF16)

    for d in range(1, 8):
        wait(att.at[0], aa_s.at[d - 1])
    for hf in range(2):
        for n in range(2):
            wait(blk(hf, 0, 0), g1_s.at[hf, n])
            wait(blk(hf, 0, 0, 0), g2_s.at[hf, n])
            for n_i in range(4):
                wait(blk(hf, 0, 0), g3_s.at[hf, n_i, n])
                wait(blk(hf, 0, 0, 0), g4_s.at[hf, n_i, n])


def on_device(stream, row_tree_nodes, gain, wqkv, adown, aup, kv, clen, parents, accepted, wo):
    vm = pl.BlockSpec(memory_space=pltpu.VMEM)
    hbm = pl.BlockSpec(memory_space=pl.ANY)
    sm = pl.BlockSpec(memory_space=pltpu.SMEM)
    dma = pltpu.SemaphoreType.DMA
    v = pltpu.VMEM
    out_t, akv = pl.pallas_call(
        kernel,
        out_shape=(
            jax.ShapeDtypeStruct((HEAD, ROWS), BF16),
            jax.ShapeDtypeStruct((2, 2, 8, COLS), BF16),
        ),
        in_specs=[hbm, vm, vm, hbm, hbm, vm, hbm, sm, vm, vm, hbm],
        out_specs=(vm, vm),
        scratch_shapes=[
            v((ROWS, WIDTH), BF16), v((56, 128), F32), v((WIDTH, RANK), BF16), v((ROWS, RANK), F32),
            v((ROWS, 128), F32), v((3, KW, COLS), BF16), v((3, KW, ASPLIT), BF16),
            v((3, KW, COLS - ASPLIT), BF16), v((2, 2, 2048, COLS), BF16), v((4, 2, 128, 3 * KW), BF16),
            v((128, 3 * KW), BF16),
            v((8, HEAD, COLS), BF16), v((UNITS, 2, 2, 4, 16, COLS), BF16),
            v((UNITS, 3, 2, 2, 16, COLS), BF16), v((UNITS, 2, 16, COLS), BF16), v((UNITS, 2, 16, COLS), F32),
            v((3, 8, 16, COLS), BF16), v((ROWS, ROWS), BF16), v((128, 128), BF16), v((128, 128), BF16),
            v((2, NODES, NODES), F32), v((2, 256, COLS), BF16), v((2, 256, COLS), F32),
            v((2, 256, 128), F32), v((2, 256, 128), F32), v((8, 16, COLS), BF16), v((8, 16, 16, COLS), BF16),
            dma((8,)), dma((9,)), dma((7,)), dma((7,)), dma((7,)), dma((3, 2)), dma((3, 2)), dma((3, UNITS)), dma((3, UNITS)),
            dma((7,)), dma((7,)), dma((2, 2)), dma((2, 2)), dma((2, 2)), dma((2,)),
            dma((2, 4, 2)), dma((2, 4, 2)), dma((2, 4, 2)), dma((2, 4)),
        ],
        compiler_params=pltpu.CompilerParams(
            collective_id=0, has_side_effects=True, vmem_limit_bytes=67043328
        ),
        name="tree_verify",
    )(
        stream, row_tree_nodes.reshape(16, 128), gain.reshape(56, 128), jnp.transpose(wqkv, (1, 0, 2)),
        adown, jnp.transpose(aup, (1, 0, 2)), kv, clen, parents, accepted, jnp.transpose(wo),
    )
    return jnp.transpose(out_t), akv


def solution(mesh):
    placed = (
        P("tok", None), P(), P(), P("head", None, "tok"), P(), P("head", None, "tok"),
        P(None, "head", None, "tok"), P("head"), P("head", None), P("head", None), P("tok", "head"),
    )
    return jax.shard_map(
        on_device, mesh=mesh, in_specs=placed,
        out_specs=(P("tok", "head"), P(None, "head", None, "tok")), check_vma=False,
    )
```

```python
import functools

import jax
import jax.numpy as jnp
from jax import lax
from jax.experimental import pallas as pl
from jax.experimental.pallas import tpu as pltpu
from jax.sharding import PartitionSpec as P

MESH = pl.DeviceIdType.MESH
F32 = jnp.float32
BF16 = jnp.bfloat16

WIDTH = 7168
COLS = 896
HEAD = 224
LOCAL_HEADS = 4
RANK = 128
NODES = 64
ROWS = 256
KW = 512
UNITS = 12
LAG = 3
SPLITS = (512, 384, 512)
SENT = 464
PIECE = 1024
WIN = 512
SPLIT = 384
NEG = float("-inf")
NT = (((1,), (1,)), ((), ()))


def iota(shape, dim):
    return lax.broadcasted_iota(jnp.int32, shape, dim)


def mm(a, b):
    return jnp.dot(a, b, preferred_element_type=F32)


def column_of(row):
    n = row.shape[1]
    eye = iota((n, n), 0) == iota((n, n), 1)
    return jnp.sum(jnp.where(eye, jnp.broadcast_to(row, (n, n)), 0.0), axis=1, keepdims=True)


def row_of(col):
    n = col.shape[0]
    eye = iota((n, n), 0) == iota((n, n), 1)
    return jnp.sum(jnp.where(eye, jnp.broadcast_to(col, (n, n)), 0.0), axis=0, keepdims=True)


def one(mask):
    return jnp.where(mask, 1.0, 0.0).astype(BF16)


def kernel(
    stream_h, nodes, gain, wqkv_h, adown_h, aup, kv_h, clen, parents, accepted, wo_h,
    out_ref, akv_ref,
    stream_v, gain32, adown_v, low_acc, rstd_v, wbuf, wa, wb, kv_v, xbuf, pack, wo_v, part,
    ra, rb, mine_sum, qkv, sort_p, node_q, node_qt, anc_v, qbd, acc_v, m_v, l_v, kn_v, vn_v, att, res,
    ld, x_s, x_r, w_s, w_r, p_s, p_r, rs_s, rs_r, aa_s, aa_r, g1_s, g1_r, g2_s, g2_r, g3_s, g3_r, g4_s, g4_r,
):
    t = lax.axis_index("tok")
    h = lax.axis_index("head")
    z, core = t // 2, t % 2
    y, x = h // 4, h % 4

    def hx(d):
        return y * 4 + (x + d + 4) % 4

    def hy(d):
        return ((y + d + 4) % 4) * 4 + x

    c1, c2 = jnp.where(core == 0, x, y), jnp.where(core == 0, y, x)
    par = c2 % 2

    def dev1(d):
        return jnp.where(core == 0, hx(d), hy(d))

    def dev2(d):
        return jnp.where(core == 0, hy(d), hx(d))

    dev_a = jnp.where(par == 0, dev2(1), dev2(-1))
    dev_b = jnp.where(par == 0, dev2(-1), dev2(1))

    def tz(d, other=False):
        c = 1 - core if other else core
        return ((z + d + 4) % 4) * 2 + c

    cm, cp, cf = (c1 + 3) % 4, (c1 + 1) % 4, (c1 + 2) % 4
    own_v = c2 // 2
    far_v = 1 - own_v

    def slot_of(tok):
        dz, same = (tok // 2 - z + 4) % 4, tok % 2 == core
        near = jnp.where(same, 2, 4) + jnp.where(dz == 1, 1, 0)
        far = jnp.where(same, 6, 7)
        return jnp.where(dz == 0, tok % 2, jnp.where(dz == 2, far, near))

    def send(src, dst, ssem, rsem, axis, idx):
        pltpu.make_async_remote_copy(
            src_ref=src, dst_ref=dst, send_sem=ssem, recv_sem=rsem,
            device_id={axis: idx}, device_id_type=MESH,
        ).start()

    def wait(ref, sem):
        pltpu.make_async_copy(ref, ref, sem).wait()

    odd = h % 2
    koff = pl.multiple_of(64 * odd, 64)
    foff = pl.multiple_of(448 - 400 * odd, 16)
    sent = pl.ds(pl.multiple_of(48 * odd, 16), SENT)
    w_c = pltpu.make_async_copy(wqkv_h, wbuf.at[:, pl.ds(koff, 448), :], ld.at[5])
    w_c.start()
    loads = []
    for r in range(4):
        c = pltpu.make_async_copy(
            stream_h.at[pl.ds(64 * r, 64)], stream_v.at[pl.ds(64 * r, 64)], ld.at[r]
        )
        c.start()
        loads.append(c)
    adown_c = pltpu.make_async_copy(adown_h, adown_v, ld.at[4])
    adown_c.start()
    wo_c = pltpu.make_async_copy(wo_h, wo_v.at[t], ld.at[6])
    wo_c.start()
    kv_c = pltpu.make_async_copy(kv_h, kv_v, ld.at[7])

    def shares(p):
        cut = SPLITS[p]
        return (
            (pl.ds(0, cut), wa.at[:, :, pl.ds(0, cut)], dev_a),
            (pl.ds(cut, COLS - cut), wb.at[:, :, pl.ds(0, COLS - cut)], dev_b),
        )

    blank = jnp.zeros((48, COLS), BF16)
    for p in range(3):
        for lo in (0, 464):
            wa[p, lo:lo + 48, :] = blank[:, :512]
            wb[p, lo:lo + 48, :] = blank[:, :512]

    bar = pltpu.get_barrier_semaphore()
    for d in range(1, 8):
        pl.semaphore_signal(bar, inc=1, device_id={"tok": (t + d) % 8}, device_id_type=MESH)
    for idx in (hx(1), hx(-1), hx(2), hy(1), hy(-1), hy(2)):
        pl.semaphore_signal(bar, inc=1, device_id={"head": idx}, device_id_type=MESH)

    for p in range(3):
        up = jnp.concatenate([aup[p].astype(F32), jnp.zeros((8, COLS), F32)], axis=0).astype(BF16)
        wbuf[p, pl.ds(pl.multiple_of(464 * (1 - odd), 16), 48), :] = blank
        wbuf[p, pl.ds(foff, 16), :] = up

    mine = nodes[pl.ds(2 * t, 2), :].astype(F32)
    key_row = jnp.concatenate([mine[0:1], mine[1:2]], axis=1)
    key_col = column_of(key_row)
    rank_row = jnp.sum(
        jnp.where(
            jnp.broadcast_to(key_col, (ROWS, ROWS)) < jnp.broadcast_to(key_row, (ROWS, ROWS)), 1.0, 0.0
        ),
        axis=0, keepdims=True,
    )
    sort_p[...] = one(iota((ROWS, ROWS), 0).astype(F32) == jnp.broadcast_to(rank_row, (ROWS, ROWS)))
    gain32[...] = gain[...].astype(F32)

    def finish_cut():
        for c in (wo_c, kv_c):
            c.wait()
        for p in range(3):
            wait(wa.at[p, sent], p_r.at[p, 0])
            wait(wb.at[p, sent], p_r.at[p, 1])
            for i, (_, dst, _) in enumerate(shares(p)):
                wait(dst.at[p, sent], p_s.at[p, i])
        out_ref[...] = jnp.zeros(out_ref.shape, BF16)
        akv_ref[...] = jnp.zeros(akv_ref.shape, BF16)

    pl.semaphore_wait(bar, 13)
    w_c.wait()
    for p in range(3):
        for i, (cols, dst, to) in enumerate(shares(p)):
            send(wbuf.at[p, sent, cols], dst.at[p, sent], p_s.at[p, i], p_r.at[p, i], "head", to)

    for r in range(4):
        loads[r].wait()

        def sq(kk, acc, r=r):
            blk = stream_v[pl.ds(64 * r, 64), pl.ds(pl.multiple_of(1024 * kk, 1024), 1024)].astype(F32)
            blk = blk * blk
            for b in range(8):
                acc = acc + blk[:, 128 * b:128 * b + 128]
            return acc

        acc = lax.fori_loop(0, 7, sq, jnp.zeros((64, 128), F32))
        mean = jnp.sum(acc, axis=1, keepdims=True) * (1.0 / WIDTH)
        rstd_v[pl.ds(64 * r, 64), :] = jnp.broadcast_to(lax.rsqrt(mean + 1e-5), (64, 128))
    kv_c.start()
    adown_c.wait()
    low_acc[...] = jnp.zeros((ROWS, RANK), F32)

    def low_step(kk, carry):
        parts = []
        for b in range(8):
            block = 8 * kk + b
            here = pl.ds(pl.multiple_of(128 * block, 128), 128)
            xb = stream_v[:, here].astype(F32)
            xn = (xb * rstd_v[...] * gain32[pl.ds(block, 1), :]).astype(BF16)
            stream_v[:, here] = xn
            parts.append(xn)
        low_acc[...] += mm(
            jnp.concatenate(parts, axis=1), adown_v[pl.ds(pl.multiple_of(1024 * kk, 1024), 1024), :]
        )
        return carry

    lax.fori_loop(0, 7, low_step, 0)
    low = low_acc[...].astype(BF16)

    def window(g):
        here = pl.ds(pl.multiple_of(128 * ((7 * g) // 2), 128), KW)
        spot = 448 - 400 * (g % 2)
        li = iota((RANK, KW), 1) - spot
        place = one((iota((RANK, KW), 0) - 8 * g == li) & (li >= 0) & (li < 8))
        terms = mm(low, place)
        lane = iota((ROWS, KW), 1) - 448 * (1 - g % 2)
        return jnp.where((lane >= 0) & (lane < 64), terms, stream_v[:, here].astype(F32)).astype(BF16)

    def rows_for(core_to, mine, dst):
        parity = jnp.where(core_to == 0, y % 2, x % 2)
        i = iota((128, ROWS), 0)
        i2, i1 = parity + 2 * (i // 64), (i // 16) % 4
        rank = 16 * jnp.where(core_to == 0, 4 * i2 + i1, 4 * i1 + i2) + i % 16
        pick = one(rank.astype(F32) == jnp.broadcast_to(rank_row, (128, ROWS)))
        step_a = 1 - 2 * parity
        for n, block in enumerate((None, step_a, -step_a)):
            if block is None:
                win = mine
            else:
                win = window(jnp.where(core_to == 0, ((y + block + 4) % 4) * 4 + x, y * 4 + (x + block + 4) % 4))
            dst[:, KW * n:KW * n + KW] = mm(pick, win).astype(BF16)

    mine_win = window(h)
    def x_send(src, to, si, ri, d):
        send(src, to, x_s.at[si], x_r.at[ri], "tok", tz(d))

    rows_for(core, mine_win, xbuf.at[0, core])
    x_send(xbuf.at[0, core], xbuf.at[1, 0], 0, 1, 1)
    x_send(xbuf.at[0, core], xbuf.at[1, 1], 1, 2, -1)
    rows_for(1 - core, mine_win, pack)
    send(pack, xbuf.at[0, core], x_s.at[2], x_r.at[0], "tok", tz(0, True))

    def x_mate():
        got = xbuf.at[0, 1 - core]
        wait(got, x_r.at[0])
        x_send(got, xbuf.at[2, 0], 3, 3, 1)
        x_send(got, xbuf.at[2, 1], 4, 4, -1)

    def x_relay(k):
        lo, hi = pl.ds(0, 64), pl.ds(64, 64)
        x_send(xbuf.at[k, 0, lo], xbuf.at[3, k - 1, lo], 3 + 2 * k, k + 4, 1)
        x_send(xbuf.at[k, 1, hi], xbuf.at[3, k - 1, hi], 4 + 2 * k, k + 4, -1)

    near = tuple((d, tz(d)) for d in (-1, 1, 2))

    def wo_own():
        own = wo_v.at[t]
        send(own, own, w_s.at[0], w_r.at[0], "tok", tz(0, True))
        for n, d in enumerate((1, -1, 2)):
            send(own, own, w_s.at[1 + n], w_r.at[1 + n], "tok", tz(d))

    def wo_mate():
        for n, (d, src) in enumerate(near):
            wait(wo_v.at[src], w_r.at[1 + n])
            send(wo_v.at[src], wo_v.at[src], w_s.at[4 + n], w_r.at[4 + n], "tok", tz(0, True))

    def wo_rest():
        wait(wo_v.at[t], w_r.at[0])
        for n in range(3):
            wait(wo_v.at[t], w_r.at[4 + n])
        for n in range(7):
            wait(wo_v.at[t], w_s.at[n])

    def add2(a, b):
        return a.astype(F32) + b.astype(F32)

    def s_matmul(u):
        k, p = u // 3, u % 3
        base = mm(xbuf[k, :, :, 0:KW].reshape(256, KW), wbuf[p])
        near_a = xbuf[k, :, :, KW:2 * KW].reshape(256, KW)
        near_b = xbuf[k, :, :, 2 * KW:3 * KW].reshape(256, KW)

        def finish(cut):
            a = base[:, :cut] + mm(near_a, wa[p, :, 0:cut])
            part[u, :, :, :, :, 0:cut] = a.astype(BF16).reshape(2, 2, 4, 16, cut)
            b = base[:, cut:] + mm(near_b, wb[p, :, 0:COLS - cut])
            part[u, :, :, :, :, cut:COLS] = b.astype(BF16).reshape(2, 2, 4, 16, COLS - cut)

        @pl.when(p == 1)
        def _():
            finish(SPLITS[1])

        @pl.when(p != 1)
        def _():
            finish(SPLITS[0])

        s_a1(u)

    def s_a1(u):
        ss, rr = rs_s.at[0, u], rs_r.at[0, u]
        send(part.at[u, 0, :, cf], ra.at[u, 2, 0], ss, rr, "head", dev1(1))
        send(part.at[u, 1, :, cf], ra.at[u, 2, 1], ss, rr, "head", dev1(-1))

    def s_b1(u):
        wait(ra.at[u, 2], rs_r.at[0, u])
        ss, rr = rs_s.at[2, u], rs_r.at[2, u]
        part[u, 0, :, cp] = add2(part[u, 0, :, cp], ra[u, 2, 0]).astype(BF16)
        send(part.at[u, :, :, cp], ra.at[u, 0], ss, rr, "head", dev1(1))
        part[u, 1, :, cm] = add2(part[u, 1, :, cm], ra[u, 2, 1]).astype(BF16)
        send(part.at[u, :, :, cm], ra.at[u, 1], ss, rr, "head", dev1(-1))

    def s_sum(u):
        wait(ra.at[u, 0:2], rs_r.at[2, u])
        ss, rr = rs_s.at[1, u], rs_r.at[1, u]

        def total(v):
            a = add2(part[u, :, v, c1], ra[u, 0, :, v])
            return a + ra[u, 1, :, v].astype(F32)
            return a + add2(ra[u, 1, :, v], ra[u, 2, :, v])

        part[u, :, far_v, c1] = total(far_v).astype(BF16)
        send(part.at[u, :, far_v, c1], rb.at[u], ss, rr, "head", dev2(2))
        mine_sum[u] = total(own_v)

    def s_fin(u):
        wait(rb.at[u], rs_r.at[1, u])
        k, p = u // 3, u % 3
        for e in range(2):
            qkv[p, 2 * k + e] = (mine_sum[u, e] + rb[u, e].astype(F32)).astype(BF16)

    def prepare():
        node_col = iota((128, 128), 0).astype(F32) + (128 * h).astype(F32)
        acc = jnp.zeros((128, 128), F32)
        for b in range(16):
            line = jnp.broadcast_to(nodes[b:b + 1, :].astype(F32), (128, 128))
            acc = acc + jnp.where(line == node_col, slot_of(b // 2).astype(F32), 0.0)
        slot_col = jnp.sum(acc, axis=1, keepdims=True)
        slot_row = row_of(slot_col)
        before = (jnp.broadcast_to(slot_col, (128, 128)) == jnp.broadcast_to(slot_row, (128, 128))) & (
            iota((128, 128), 1) < iota((128, 128), 0)
        )
        pos_col = 16.0 * slot_col + jnp.sum(jnp.where(before, 1.0, 0.0), axis=1, keepdims=True)
        pos_row = row_of(pos_col)
        node_qt[...] = one(iota((128, 128), 1).astype(F32) == jnp.broadcast_to(pos_col, (128, 128)))
        node_q[...] = one(iota((128, 128), 0).astype(F32) == jnp.broadcast_to(pos_row, (128, 128)))
        for r in range(2):
            up = column_of(parents[r:r + 1, :].astype(F32))
            i0, i1 = iota((NODES, NODES), 0), iota((NODES, NODES), 1)
            anc = one((i0 == i1) | (i1.astype(F32) == jnp.broadcast_to(up, (NODES, NODES))))
            for _ in range(6):
                anc = jnp.minimum(mm(anc, anc), 1.0).astype(BF16)
            anc_v[r] = anc.astype(F32)
        m_v[...] = jnp.full(m_v.shape, NEG, F32)
        l_v[...] = jnp.zeros(l_v.shape, F32)
        acc_v[...] = jnp.zeros(acc_v.shape, F32)

    def in_nodes(p):
        return mm(node_qt[...], qkv[p].reshape(128, COLS))

    def heads_in(pair):
        return (iota((NODES, WIN), 1) + SPLIT * pair) // HEAD

    def spread_queries():
        q = in_nodes(0)
        for pair in range(2):
            head_of = heads_in(pair)
            for r in range(2):
                qr = q[NODES * r:NODES * r + NODES, SPLIT * pair:SPLIT * pair + WIN]
                for j in range(2):
                    qbd[pair, r, NODES * j:NODES * j + NODES, :] = jnp.where(
                        head_of == 2 * pair + j, qr, 0.0
                    ).astype(BF16)

    scale = HEAD ** -0.5

    def soften(pair, r, s, values):
        m_old = m_v[pair, r]
        m_new = jnp.maximum(m_old, jnp.broadcast_to(jnp.max(s, axis=1, keepdims=True), m_old.shape))
        shrink = jnp.exp(m_old - m_new)
        e = jnp.exp(s - m_new[:, 0:1])
        m_v[pair, r] = m_new
        l_v[pair, r] = l_v[pair, r] * shrink + jnp.broadcast_to(jnp.sum(e, axis=1, keepdims=True), m_old.shape)
        acc_v[pair, r] = acc_v[pair, r] * shrink[:, 0:1] + mm(e.astype(BF16), values)

    def cache_piece(pair, i):
        r, c = i // 2, i % 2
        here = pl.ds(pl.multiple_of(PIECE * c, PIECE), PIECE)
        cols = pl.ds(SPLIT * pair, WIN)
        s = lax.dot_general(qbd[pair, r], kv_v[0, r, here, cols], NT, preferred_element_type=F32) * scale
        live = iota((128, PIECE), 1) + PIECE * c < clen[r]
        soften(pair, r, jnp.where(live, s, NEG), kv_v[1, r, here, cols])

    start_att = 9 + (3) * LAG
    last = start_att + 4

    def body(it, carry):
        stages = ((3 * LAG, s_fin), (2 * LAG, s_sum), (LAG, s_b1))
        for lag, stage in stages:
            @pl.when((it >= lag) & (it < UNITS + lag))
            def _(lag=lag, stage=stage):
                stage(it - lag)

        @pl.when(it < UNITS)
        def _():
            for p in range(3):
                @pl.when(it == p)
                def _(p=p):
                    for i, (_, dst, _) in enumerate(shares(p)):
                        wait(dst.at[p, sent], p_r.at[p, i])

            @pl.when(it == 0)
            def _():
                x_mate()

            @pl.when((it == 3) | (it == 6) | (it == 9))
            def _():
                k = it // 3
                wait(xbuf.at[k, 0], x_r.at[2 * k - 1])
                wait(xbuf.at[k, 1], x_r.at[2 * k])
                @pl.when(it < 9)
                def _():
                    x_relay(k)

            s_matmul(it)

        @pl.when(it == 1)
        def _():
            prepare()

        @pl.when(it == 8)
        def _():
            wo_c.wait()
            wo_own()

        @pl.when(it == start_att + 3)
        def _():
            wo_mate()

        @pl.when(it == start_att)
        def _():
            kv_c.wait()
            spread_queries()

        @pl.when(it >= start_att)
        def _():
            cache_piece(0, it - start_att)

        return carry

    lax.fori_loop(0, last, body, 0)

    def drain_rs():
        for i in range(5):
            wait(xbuf.at[0, 0], x_s.at[i])
        for i in range(5, 9):
            wait(xbuf.at[0, 0, pl.ds(0, 64)], x_s.at[i])
        wo_rest()
        for p in range(3):
            for i, (_, dst, _) in enumerate(shares(p)):
                wait(dst.at[p, sent], p_s.at[p, i])

        def drain(u, carry):
            for k, ref in enumerate((ra.at[:, 2], rb, ra.at[:, 0:2])):
                wait(ref.at[u], rs_s.at[k, u])
            return carry

        lax.fori_loop(0, UNITS, drain, 0)

    kn_v[...] = in_nodes(1).astype(BF16)
    vn_v[...] = in_nodes(2).astype(BF16)

    def tree(pair):
        outs = []
        head_of = heads_in(pair)
        for r in range(2):
            rows = pl.ds(NODES * r, NODES)
            cols = pl.ds(SPLIT * pair, WIN)
            s = lax.dot_general(qbd[pair, r], kn_v[rows, cols], NT, preferred_element_type=F32) * scale
            keep = jnp.concatenate([anc_v[r]] * 2, axis=0) > 0.5
            soften(pair, r, jnp.where(keep, s, NEG), vn_v[rows, cols])
            norm = acc_v[pair, r] / l_v[pair, r][:, 0:1]
            outs.append(jnp.where(head_of == 2 * pair, norm[0:NODES], norm[NODES:2 * NODES]))
        return jnp.concatenate(outs, axis=0).astype(BF16)

    lanes = (pl.ds(0, SPLIT), pl.ds(SPLIT, WIN))

    def home_sends(c):
        for d in range(1, 8):
            to = (t + d) % 8
            send(
                att.at[slot_of(to), :, lanes[c]], res.at[t, h, :, lanes[c]],
                aa_s.at[c, d - 1], aa_r.at[c, d - 1], "tok", to,
            )
        res[t, h, :, lanes[c]] = att[core, :, lanes[c]]

    def home_waits(c):
        for d in range(1, 8):
            wait(res.at[(t - d + 8) % 8, h, :, lanes[c]], aa_r.at[c, d - 1])

    steps = (0, -1, 1, 2)

    def slot(hf, i, j):
        if hf == 0:
            return ((y + j + 4) % 4) * 4 + (x + i + 4) % 4
        return ((y + i + 4) % 4) * 4 + (x + j + 4) % 4

    def blk(c, hf, i, j, part_of=None):
        lo, n = (4 * hf, 4) if part_of is None else (4 * hf + 2 * part_of, 2)
        return res.at[pl.ds(lo, n), slot(hf, i, j), :, lanes[c]]

    def dev(hf, axis, d):
        return slot(hf, d, 0) if axis == 0 else slot(hf, 0, d)

    def cross_sends(c, hf, n_i):
        b = blk(c, hf, steps[n_i], 0)
        for n, d in enumerate((1, -1)):
            send(b, b, g3_s.at[c, hf, n_i, n], g3_r.at[c, hf, n_i, n], "head", dev(hf, 1, d))

    def cross_forward(c, n_i):
        i = steps[n_i]
        for hf in range(2):
            for n, d in enumerate((1, -1)):
                wait(blk(c, hf, i, -d), g3_r.at[c, hf, n_i, n])
                b = blk(c, hf, i, -d, n)
                send(b, b, g4_s.at[c, hf, n_i, n], g4_r.at[c, hf, n_i], "head", dev(hf, 1, d))

    def gather_first(c):
        for hf in range(2):
            b = blk(c, hf, 0, 0)
            for n, d in enumerate((1, -1)):
                send(b, b, g1_s.at[c, hf, n], g1_r.at[c, hf, n], "head", dev(hf, 0, d))
        for hf in range(2):
            cross_sends(c, hf, 0)

    def gather_second(c):
        for hf in range(2):
            for n, d in enumerate((1, -1)):
                wait(blk(c, hf, -d, 0), g1_r.at[c, hf, n])
                b = blk(c, hf, -d, 0, n)
                send(b, b, g2_s.at[c, hf, n], g2_r.at[c, hf], "head", dev(hf, 0, d))
                cross_sends(c, hf, 1 + n)

    def gather_third(c):
        for hf in range(2):
            wait(blk(c, hf, 2, 0), g2_r.at[c, hf])
            cross_sends(c, hf, 3)

    def gather_end(c):
        for hf in range(2):
            for n_i in range(4):
                wait(blk(c, hf, steps[n_i], 2), g4_r.at[c, hf, n_i])

    def project(c):
        total = jnp.zeros((HEAD, ROWS), F32)
        width = (SPLIT, WIN)[c]
        for s in range(8):
            total = total + lax.dot_general(
                wo_v[s, :, lanes[c]], res[s, :, :, lanes[c]].reshape(ROWS, width), NT, preferred_element_type=F32
            )
        return total

    o0 = tree(0)
    att[:, :, 0:SPLIT] = mm(node_q[...], o0[:, 0:SPLIT]).astype(BF16).reshape(8, 16, SPLIT)
    home_sends(0)

    def second(i, carry):
        cache_piece(1, i)
        return carry

    lax.fori_loop(0, 4, second, 0)
    home_waits(0)
    gather_first(0)
    o1 = tree(1)
    first_lanes = jnp.where(
        iota((128, 128), 1) < 2 * HEAD - SPLIT, o0[:, SPLIT:WIN].astype(F32), o1[:, 0:128].astype(F32)
    ).astype(BF16)
    o1 = jnp.concatenate([first_lanes, o1[:, 128:WIN]], axis=1)
    att[:, :, SPLIT:COLS] = mm(node_q[...], o1).astype(BF16).reshape(8, 16, WIN)
    home_sends(1)
    gather_second(0)
    for r in range(2):
        col = column_of(accepted[r:r + 1, :].astype(F32)) + float(NODES * r)
        pick = one(iota((8, 128), 1).astype(F32) == jnp.broadcast_to(col, (8, 128)))
        akv_ref[0, r] = mm(pick, kn_v[...]).astype(BF16)
        akv_ref[1, r] = mm(pick, vn_v[...]).astype(BF16)
    home_waits(1)
    gather_first(1)
    cross_forward(0, 0)
    gather_third(0)
    cross_forward(0, 1)
    cross_forward(0, 2)
    gather_second(1)
    cross_forward(0, 3)
    cross_forward(1, 0)
    gather_third(1)
    drain_rs()
    gather_end(0)
    cross_forward(1, 1)
    cross_forward(1, 2)
    half = project(0)
    cross_forward(1, 3)
    gather_end(1)
    total = half + project(1)
    out_ref[...] = mm(total.astype(BF16), sort_p[...]).astype(BF16)

    for c in range(2):
        for d in range(1, 8):
            wait(att.at[0, :, lanes[c]], aa_s.at[c, d - 1])
        for hf in range(2):
            for n in range(2):
                wait(blk(c, hf, 0, 0), g1_s.at[c, hf, n])
                wait(blk(c, hf, 0, 0, 0), g2_s.at[c, hf, n])
                for n_i in range(4):
                    wait(blk(c, hf, 0, 0), g3_s.at[c, hf, n_i, n])
                    wait(blk(c, hf, 0, 0, 0), g4_s.at[c, hf, n_i, n])


def hand_out(a_ref, b_ref, a_out, b_out):
    a_out[...] = a_ref[...]
    b_out[...] = b_ref[...]


def on_device(stream, row_tree_nodes, gain, wqkv, adown, aup, kv, clen, parents, accepted, wo):
    vm = pl.BlockSpec(memory_space=pltpu.VMEM)
    hbm = pl.BlockSpec(memory_space=pl.ANY)
    sm = pl.BlockSpec(memory_space=pltpu.SMEM)
    dma = pltpu.SemaphoreType.DMA
    v = pltpu.VMEM
    out_t, akv = pl.pallas_call(
        kernel,
        out_shape=(
            jax.ShapeDtypeStruct((HEAD, ROWS), BF16),
            jax.ShapeDtypeStruct((2, 2, 8, COLS), BF16),
        ),
        in_specs=[hbm, vm, vm, hbm, hbm, vm, hbm, sm, vm, vm, hbm],
        out_specs=(vm, vm),
        scratch_shapes=[
            v((ROWS, WIDTH), BF16), v((56, 128), F32), v((WIDTH, RANK), BF16), v((ROWS, RANK), F32),
            v((ROWS, 128), F32), v((3, KW, COLS), BF16), v((3, KW, 512), BF16),
            v((3, KW, 512), BF16), v((2, 2, 2048, COLS), BF16), v((4, 2, 128, 3 * KW), BF16),
            v((128, 3 * KW), BF16),
            v((8, HEAD, COLS), BF16), v((UNITS, 2, 2, 4, 16, COLS), BF16),
            v((UNITS, 3, 2, 2, 16, COLS), BF16), v((UNITS, 2, 16, COLS), BF16), v((UNITS, 2, 16, COLS), F32),
            v((3, 8, 16, COLS), BF16), v((ROWS, ROWS), BF16), v((128, 128), BF16), v((128, 128), BF16),
            v((2, NODES, NODES), F32), v((2, 2, 128, WIN), BF16), v((2, 2, 128, WIN), F32),
            v((2, 2, 128, 128), F32), v((2, 2, 128, 128), F32), v((128, COLS), BF16), v((128, COLS), BF16), v((8, 16, COLS), BF16), v((8, 16, 16, COLS), BF16),
            dma((8,)), dma((9,)), dma((7,)), dma((7,)), dma((7,)), dma((3, 2)), dma((3, 2)), dma((3, UNITS)), dma((3, UNITS)),
            dma((2, 7)), dma((2, 7)), dma((2, 2, 2)), dma((2, 2, 2)), dma((2, 2, 2)), dma((2, 2)),
            dma((2, 2, 4, 2)), dma((2, 2, 4, 2)), dma((2, 2, 4, 2)), dma((2, 2, 4)),
        ],
        compiler_params=pltpu.CompilerParams(
            collective_id=0, has_side_effects=True, vmem_limit_bytes=67043328
        ),
        name="tree_verify",
    )(
        stream, row_tree_nodes.reshape(16, 128), gain.reshape(56, 128), jnp.transpose(wqkv, (1, 0, 2)),
        adown, jnp.transpose(aup, (1, 0, 2)), kv, clen, parents, accepted, jnp.transpose(wo),
    )
    out_t, akv = pl.pallas_call(
        hand_out,
        out_shape=(jax.ShapeDtypeStruct(out_t.shape, BF16), jax.ShapeDtypeStruct(akv.shape, BF16)),
        in_specs=[vm, vm],
        out_specs=(vm, vm),
        name="hand_out",
    )(out_t, akv)
    return jnp.transpose(out_t), akv


def solution(mesh):
    placed = (
        P("tok", None), P(), P(), P("head", None, "tok"), P(), P("head", None, "tok"),
        P(None, "head", None, "tok"), P("head"), P("head", None), P("head", None), P("tok", "head"),
    )
    return jax.shard_map(
        on_device, mesh=mesh, in_specs=placed,
        out_specs=(P("tok", "head"), P(None, "head", None, "tok")), check_vma=False,
    )
```
